512 devices in a mesh: ctx: 32 (over z_hi, x, core), head: 16 (over y, z_lo).
Axes of the slice: x: 4, y: 8, z: 8 (z_hi: 4, z_lo: 2; z = z_hi * 2 + z_lo), core: 2. Of those that a mesh axis runs over, the one named last changes fastest.
Arguments:
- queries: bfloat16 [32768, 2048], P('ctx', 'head'), may hold values from -4.5 to 4.5
- keys: bfloat16 [32768, 2048], P('ctx', 'head'), may hold values from -4.5 to 4.5
- values: bfloat16 [32768, 2048], P('ctx', 'head'), may hold values from -6 to 6
- out_weight: bfloat16 [2048, 2048], P('head'), may hold values from -0.5 to 0.5
Outputs:
- mixed: bfloat16 [32768, 2048], P(('ctx', 'head'))
The draws below stay inside these ranges and needn't reach their ends.
All inputs are finite; a program needn't handle non-finite values.
Results may differ from the reference program's by a relative error of at most 0.019.
Values may be sent and summed in bfloat16 or wider, within the bound.
A program may use at most 64 MiB of HBM per device.

```python
import jax
import jax.numpy as jnp
from jax import lax

D = 2048
HEADS = 16
HEAD_SIZE = 128
WINDOW = 512
STRIDE = 16
BLOCK = 128
SUMCOLS = 8
SEQUENCE_TOKENS = 32768
N_HEAD = 16


def drawn_pair(key):
    width = HEADS * HEAD_SIZE
    query_seed = jax.random.fold_in(key, 101)
    keys_seed = jax.random.fold_in(key, 202)
    query_draw = jnp.clip(jax.random.normal(query_seed, (SEQUENCE_TOKENS, width), jnp.float32), -4.5, 4.5)
    keys_draw = jnp.clip(jax.random.normal(keys_seed, (SEQUENCE_TOKENS, width), jnp.float32), -4.5, 4.5)
    return (query_draw, keys_draw)


def draw_queries(key, part):
    return drawn_pair(key)[0].astype(jnp.bfloat16)


def draw_keys(key, part):
    return drawn_pair(key)[1].astype(jnp.bfloat16)


def block_levels(rng, dims, shards, low, largest):
    def one(dim, shards_of):
        draws = jax.random.uniform(jax.random.fold_in(jax.random.fold_in(rng, 6), dim), (shards_of,), jnp.float32, low / len(shards), largest / len(shards))
        return jnp.repeat(jnp.exp(draws), dims[dim] // shards_of).reshape((-1,) + (1,) * (len(dims) - dim - 1))

    loudness = one(*shards[0])
    for cut in shards[1:]:
        loudness = loudness * one(*cut)
    return loudness


def bell_draw(stream_key, shape, scale, most, shards=(), held_as=jnp.bfloat16):
    values = jax.random.normal(stream_key, shape, jnp.float32) * scale
    if len(shards) > 0:
        values = block_levels(stream_key, shape, shards, -0.22, 0.18) * values
    return jnp.clip(values, min=-most, max=most).astype(held_as)


def setup_inputs(seed: int = 0) -> dict:
    streams_of = jax.random.split(jax.random.key(seed), 5)
    return {
        "queries": draw_queries(jax.random.fold_in(streams_of[4], 71), 0),
        "keys": draw_keys(jax.random.fold_in(streams_of[4], 71), 0),
        "values": bell_draw(streams_of[2], (SEQUENCE_TOKENS, HEADS * HEAD_SIZE), 1.0, 6.0, ((0, 32), (1, 16))),
        "out_weight": bell_draw(streams_of[3], (HEADS * HEAD_SIZE, D), HEAD_SIZE ** -0.5, 0.5, ((0, 16),)),
    }


BIG_NEG = -1e30


def to_float(array):
    return array.astype(jnp.float32)


def round_trip(array):
    return lax.optimization_barrier(array.astype(jnp.bfloat16)).astype(jnp.float32)


def softmax_weighted(logit_scores, permitted_mask, value_rows, form):
    masked = jnp.where(permitted_mask, logit_scores, BIG_NEG)
    row_top = jnp.max(masked, axis=-1, keepdims=True)
    exponent = jnp.where(permitted_mask, jnp.exp(masked - row_top), 0.0)
    total = jnp.sum(exponent, axis=-1, keepdims=True)
    return jnp.einsum(form, round_trip(exponent), value_rows) / total


def local_head(query, key_rows, value_rows):
    score_scale = HEAD_SIZE ** -0.5
    blocks = SEQUENCE_TOKENS // WINDOW
    query_block_rows = to_float(query).reshape(blocks, WINDOW, HEAD_SIZE)
    padding = jnp.zeros((WINDOW, HEAD_SIZE), jnp.float32)
    key_ext = jnp.concatenate([padding, to_float(key_rows)]).reshape(blocks + 1, WINDOW, HEAD_SIZE)
    value_ext = jnp.concatenate([padding, to_float(value_rows)]).reshape(blocks + 1, WINDOW, HEAD_SIZE)
    paired_keys = jnp.concatenate([key_ext[:-1], key_ext[1:]], axis=1)
    paired_values = jnp.concatenate([value_ext[:-1], value_ext[1:]], axis=1)
    logit_scores = jnp.einsum("vix,vox->vio", query_block_rows, paired_keys) * score_scale
    block_ids = jnp.arange(blocks)[:, None, None]
    row_ids = jnp.arange(WINDOW)[None, :, None]
    col_ids = jnp.arange(2 * WINDOW)[None, None, :]
    query_pos = block_ids * WINDOW + row_ids
    key_pos = (block_ids - 1) * WINDOW + col_ids
    permitted_mask = (key_pos <= query_pos) & (key_pos > query_pos - WINDOW) & (key_pos >= 0)
    return softmax_weighted(logit_scores, permitted_mask, paired_values, "vzw,vwf->vzf").reshape(SEQUENCE_TOKENS, HEAD_SIZE)


def stride_head(query, key_rows, value_rows):
    score_scale = HEAD_SIZE ** -0.5
    row_count = SEQUENCE_TOKENS // STRIDE
    query_phase = to_float(query).reshape(row_count, STRIDE, HEAD_SIZE).transpose(1, 0, 2)
    key_phase = to_float(key_rows).reshape(row_count, STRIDE, HEAD_SIZE).transpose(1, 0, 2)
    value_phase = to_float(value_rows).reshape(row_count, STRIDE, HEAD_SIZE).transpose(1, 0, 2)
    order = jnp.arange(row_count)
    permitted_mask = order[None, :] <= order[:, None]

    def one_phase(operands):
        phase_query, phase_keys, phase_values = operands
        logit_scores = jnp.einsum("qd,kd->qk", phase_query, phase_keys) * score_scale
        return softmax_weighted(logit_scores, permitted_mask, phase_values, "qk,kd->qd")

    result = lax.map(one_phase, (query_phase, key_phase, value_phase))
    return result.transpose(1, 0, 2).reshape(SEQUENCE_TOKENS, HEAD_SIZE)


def summary_head(query, key_rows, value_rows):
    score_scale = HEAD_SIZE ** -0.5
    total_keys = SEQUENCE_TOKENS // BLOCK * SUMCOLS
    key_sum = to_float(key_rows).reshape(SEQUENCE_TOKENS // BLOCK, BLOCK, HEAD_SIZE)[:, BLOCK - SUMCOLS:].reshape(total_keys, HEAD_SIZE)
    value_sum = to_float(value_rows).reshape(SEQUENCE_TOKENS // BLOCK, BLOCK, HEAD_SIZE)[:, BLOCK - SUMCOLS:].reshape(total_keys, HEAD_SIZE)
    index = jnp.arange(total_keys)
    key_pos = index // SUMCOLS * BLOCK + BLOCK - SUMCOLS + index % SUMCOLS
    step_rows = min(SEQUENCE_TOKENS, 512)
    count_blocks = SEQUENCE_TOKENS // step_rows
    query_block_rows = to_float(query).reshape(count_blocks, step_rows, HEAD_SIZE)
    key_blocks = to_float(key_rows).reshape(count_blocks, step_rows, HEAD_SIZE)
    value_blocks = to_float(value_rows).reshape(count_blocks, step_rows, HEAD_SIZE)

    def one_block(operands):
        number, block_query, block_keys, block_values = operands
        query_pos = number * step_rows + jnp.arange(step_rows)
        logit_scores = jnp.einsum("qd,kd->qk", block_query, key_sum) * score_scale
        permitted_mask = key_pos[None, :] <= query_pos[:, None]
        own_score = jnp.sum(block_query * block_keys, axis=-1) * score_scale
        own_allowed = query_pos % BLOCK < BLOCK - SUMCOLS
        masked = jnp.where(permitted_mask, logit_scores, BIG_NEG)
        own_masked = jnp.where(own_allowed, own_score, BIG_NEG)
        row_top = jnp.maximum(jnp.max(masked, axis=-1), own_masked)
        exponent = jnp.where(permitted_mask, jnp.exp(masked - row_top[:, None]), 0.0)
        own_exponent = jnp.where(own_allowed, jnp.exp(own_masked - row_top), 0.0)
        total = jnp.sum(exponent, axis=-1) + own_exponent
        result = jnp.einsum("qk,kd->qd", round_trip(exponent), value_sum)
        result = result + round_trip(own_exponent)[:, None] * block_values
        return result / total[:, None]

    result = lax.map(one_block, (jnp.arange(count_blocks), query_block_rows, key_blocks, value_blocks))
    return result.reshape(SEQUENCE_TOKENS, HEAD_SIZE)


def reference(queries, keys, values, out_weight):
    def split_heads(array):
        return array.reshape(SEQUENCE_TOKENS, HEADS, HEAD_SIZE).transpose(1, 0, 2)

    def per_head(operands):
        query, key_rows, value_rows = operands
        return local_head(query, key_rows, value_rows) + stride_head(query, key_rows, value_rows) + summary_head(query, key_rows, value_rows)

    sections = lax.map(per_head, (split_heads(queries), split_heads(keys), split_heads(values)))
    attended = sections.transpose(1, 0, 2).reshape(SEQUENCE_TOKENS, HEADS * HEAD_SIZE).astype(jnp.bfloat16)
    group_width = HEADS // N_HEAD * HEAD_SIZE
    attended_groups = attended.reshape(SEQUENCE_TOKENS, N_HEAD, group_width).transpose(1, 0, 2)
    weight_groups = out_weight.reshape(N_HEAD, group_width, D)

    def add_group(carry, operands):
        group_rows, group_weight = operands
        partial_value = jnp.dot(group_rows, group_weight, preferred_element_type=jnp.float32)
        return carry + round_trip(partial_value), None

    summed, unused = lax.scan(add_group, jnp.zeros((SEQUENCE_TOKENS, D), jnp.float32), (attended_groups, weight_groups))
    return summed.astype(jnp.bfloat16)
```

```python
import functools
import math

import jax
import jax.numpy as jnp
from jax import lax
from jax.experimental import pallas as pl
from jax.experimental.pallas import tpu as pltpu
from jax.sharding import PartitionSpec as P

MESH = pl.DeviceIdType.MESH
NEG = -1e30
HEAD_SIZE = 128
WINDOW = 512
LOGIT = math.log2(math.e) * HEAD_SIZE ** -0.5
F32 = jnp.float32
BF16 = jnp.bfloat16
TOKENS = 1024
CHIPS = 16
ROWS = 64
LT = 256
SPAN = LT + WINDOW


def scores(q, k):
    return lax.dot_general(q, k, (((1,), (1,)), ((), ())), preferred_element_type=F32)


def mix(p, v):
    return jnp.dot(p.astype(BF16), v, preferred_element_type=F32)


def fold(q, k, v, state, allowed=None):
    top, total, acc = state
    s = scores(q, k)
    if allowed is not None:
        s = jnp.where(allowed, s, NEG)
    new_top = jnp.maximum(top, jnp.max(s, axis=-1, keepdims=True))
    p = jnp.exp2((s - new_top) * LOGIT)
    shrink = jnp.exp2((top - new_top) * LOGIT)
    total = shrink * total + jnp.sum(p, axis=-1, keepdims=True)
    acc = shrink * acc + mix(p, v)
    return new_top, total, acc


def iota(shape, dim):
    return lax.broadcasted_iota(jnp.int32, shape, dim)


def kernel(
    q_hbm, k_hbm, v_hbm, w_hbm, out_ref,
    q, kv, stage, rq, rkv, own_sum, summ, ls, ret_out, ret, att_out, att, wbuf,
    in_sem, bar_unused, halo_sem, q_send, q_recv, kv_send, kv_recv, pair_send, pair_recv,
    sz_send, sz_recv, sx_send, sx_recv, sp_send, sp_recv,
    wz_sem, wy_send, wy_recv, wp_send, wp_recv,
    r_send, r_recv, a_send, a_recv,
):
    c = lax.axis_index("ctx")
    h = lax.axis_index("head")
    core, x, zh = c % 2, (c // 2) % 4, c // 8
    zl, y = h % 2, h // 2
    chip = zh * 4 + x
    sib = c + 1 - 2 * core
    sends = []

    def remote(src, dst, ssem, rsem, dev):
        return pltpu.make_async_remote_copy(
            src_ref=src, dst_ref=dst, send_sem=ssem, recv_sem=rsem,
            device_id=dev, device_id_type=MESH,
        )

    def go(copy):
        copy.start()
        sends.append(copy)
        return copy

    def chip_at(dz, dx):
        return ((zh + dz) % 4) * 4 + (x + dx) % 4

    offs = [(dz, dx) for dz in (2, 1, 3, 0) for dx in (2, 1, 3, 0) if dz or dx]
    heads = [(dy, dz) for dy in (4, 3, 5, 2, 6, 1, 7, 0) for dz in (1, 0) if dy or dz]

    loads = [
        pltpu.make_async_copy(q_hbm, q, in_sem.at[0]),
        pltpu.make_async_copy(k_hbm, kv.at[0, pl.ds(WINDOW, TOKENS)], in_sem.at[1]),
        pltpu.make_async_copy(v_hbm, kv.at[1, pl.ds(WINDOW, TOKENS)], in_sem.at[2]),
        pltpu.make_async_copy(w_hbm, wbuf.at[h], in_sem.at[3]),
    ]
    for load in loads:
        load.start()

    barrier = pltpu.get_barrier_semaphore()

    def greet(dev):
        pl.semaphore_signal(barrier, inc=1, device_id=dev, device_id_type=MESH)

    for dz, dx in offs:
        greet((chip_at(dz, dx) * 2 + core, h))
    for dy, dz in heads:
        greet((c, ((y + dy) % 8) * 2 + (zl + dz) % 2))
    greet((sib, h))
    greet(((c + 2 * core - 1) % 32, h))

    for load in loads[:3]:
        load.wait()

    ri, ci = iota((256, 256), 0), iota((256, 256), 1)
    swap = jnp.where(((ri >> 4) == (ci & 15)) & ((ri & 15) == (ci >> 4)), 1.0, 0.0).astype(BF16)
    for n in range(3):
        for b in range(4):
            if n == 0:
                rows = q[pl.ds(256 * b, 256), :]
            else:
                rows = kv[n - 1, pl.ds(WINDOW + 256 * b, 256), :]
            moved = jnp.dot(swap, rows, preferred_element_type=F32).astype(BF16)
            stage[:, n, pl.ds(16 * b, 16), :] = moved.reshape(CHIPS, 16, HEAD_SIZE)
    for n in range(2):
        parts = [
            kv[n, pl.ds(WINDOW + 128 * g + 112, 16), :].astype(F32)[8:] for g in range(8)
        ]
        own_sum[n] = jnp.concatenate(parts, axis=0).astype(BF16)

    rr, cc = iota((LT, SPAN), 0), iota((LT, SPAN), 1)

    def local_tile(i, bias):
        qs = q[pl.ds(pl.multiple_of(i * LT, LT), LT), :]
        window = pl.ds(pl.multiple_of(i * LT, LT), SPAN)
        s = scores(qs, kv[0, window, :])
        allowed = (cc > rr) & (cc <= rr + WINDOW)
        if bias:
            start = jnp.where(c == 0, WINDOW - i * LT, 0)
            allowed = allowed & (cc >= start)
        s = jnp.where(allowed, s, NEG)
        top = jnp.max(s, axis=-1, keepdims=True)
        p = jnp.exp2((s - top) * LOGIT)
        total = jnp.sum(p, axis=-1, keepdims=True)
        ls[pl.ds(pl.multiple_of(i * LT, LT), LT), :] = mix(p, kv[1, window, :]) / total

    half = WINDOW // LT

    @pl.loop(half, TOKENS // LT)
    def _(i):
        local_tile(i, False)

    pl.semaphore_wait(barrier, 32)

    def w_unit(yy, zz, k):
        return wbuf.at[2 * (yy % 8) + zz % 2, pl.ds(pl.multiple_of(64 * k, 64), 64), :]

    for n, dz in enumerate((2, 1, 3)):
        dev = (((zh + dz) % 4) * 8 + x * 2 + core, h)
        go(remote(own_sum, summ.at[:, zh, x, core], sz_send.at[n], sz_recv.at[n], dev))
    loads[3].wait()
    zpeer = (c, 2 * y + 1 - zl)
    go(remote(w_unit(y, zl, core), w_unit(y, zl, core), wz_sem.at[0], wz_sem.at[1], zpeer))

    def w_dev(d):
        return (c, 2 * ((y + (1, -1)[d]) % 8) + zl)

    def w_name(d, i):
        step = i // 2
        kind = (zl, 1 - zl)[i % 2] if i < 6 else (zl, 1 - zl)[d]
        return (y - (1, -1)[d] * step + 8, kind)

    def w_send(d, i):
        yy, zz = w_name(d, i)
        ref = w_unit(yy, zz, core)
        go(remote(ref, ref, wy_send.at[d, i], wy_recv.at[d, i], w_dev(d)))

    def w_pair(yy, zz, n):
        ref = w_unit(yy, zz, core)
        go(remote(ref, ref, wp_send.at[n], wp_recv.at[n], (sib, h)))

    def w_wait(d, i):
        yy, zz = w_name(d, i)
        yy = yy - (1, -1)[d]
        ref = w_unit(yy + 8, zz, core)
        remote(ref, ref, wy_send.at[d, i], wy_recv.at[d, i], w_dev(d)).wait_recv()
        return yy + 8, zz

    def w_relay(i):
        for d in range(2):
            yy, zz = w_wait(d, i)
            if i < 4:
                w_send(d, i + 2)
            elif i == 4 and d == 0 or i == 5 and d == 1:
                w_send(d, 6)
            w_pair(yy, zz, 1 + 7 * d + i)

    w_send(0, 0)
    w_send(1, 0)
    next_dev = ((c + 1) % 32, h)
    go(remote(
        kv.at[:, pl.ds(TOKENS, WINDOW)], kv.at[:, pl.ds(0, WINDOW)],
        halo_sem.at[0], halo_sem.at[1], next_dev,
    ))
    for n, (dz, dx) in enumerate(offs):
        to = chip_at(dz, dx)
        go(remote(stage.at[to, pl.ds(1, 2)], rkv.at[:, chip, core], kv_send.at[n], kv_recv.at[n], (to * 2 + core, h)))
    for n, (dz, dx) in enumerate(offs):
        to = chip_at(dz, dx)
        go(remote(stage.at[to, 0], rq.at[chip], q_send.at[n], q_recv.at[n], (to * 2 + core, h)))
    own = [
        pltpu.make_async_copy(stage.at[chip, pl.ds(1, 2)], rkv.at[:, chip, core], in_sem.at[4]),
        pltpu.make_async_copy(stage.at[chip, 0], rq.at[chip], in_sem.at[5]),
        pltpu.make_async_copy(own_sum, summ.at[:, zh, x, core], in_sem.at[6]),
    ]
    for copy in own:
        copy.start()
    go(remote(stage.at[chip, pl.ds(1, 2)], rkv.at[:, chip, core], pair_send.at[15], pair_recv.at[15], (sib, h)))

    remote(
        kv.at[:, pl.ds(TOKENS, WINDOW)], kv.at[:, pl.ds(0, WINDOW)],
        halo_sem.at[0], halo_sem.at[1], next_dev,
    ).wait_recv()

    @pl.loop(0, half)
    def _(i):
        local_tile(i, True)

    own[2].wait()
    for n, dz in enumerate((2, 1, 3)):
        ref = summ.at[:, (zh - dz + 4) % 4, x, core]
        remote(own_sum, ref, sz_send.at[n], sz_recv.at[n], (c, h)).wait_recv()
    for n, dx in enumerate((2, 1, 3)):
        dev = (zh * 8 + ((x + dx) % 4) * 2 + core, h)
        ref = summ.at[:, :, x, core]
        go(remote(ref, ref, sx_send.at[n], sx_recv.at[n], dev))
    ref = summ.at[:, :, x, core]
    go(remote(ref, ref, sp_send.at[3], sp_recv.at[3], (sib, h)))

    ref = w_unit(y, 1 - zl, core)
    remote(ref, ref, wz_sem.at[0], wz_sem.at[1], zpeer).wait_recv()
    w_send(0, 1)
    w_send(1, 1)
    w_pair(y, 1 - zl, 0)

    for n, dx in enumerate((2, 1, 3)):
        ref = summ.at[:, :, (x - dx + 4) % 4, core]
        remote(ref, ref, sx_send.at[n], sx_recv.at[n], (c, h)).wait_recv()
        go(remote(ref, ref, sp_send.at[n], sp_recv.at[n], (sib, h)))
    for n, dx in enumerate((2, 1, 3, 0)):
        ref = summ.at[:, :, (x - dx + 4) % 4, 1 - core]
        remote(ref, ref, sp_send.at[n], sp_recv.at[n], (sib, h)).wait_recv()

    def take_pairs(part):
        for n in part:
            dz, dx = offs[n]
            ref = rkv.at[:, ((zh - dz + 4) % 4) * 4 + (x - dx + 4) % 4, core]
            remote(ref, ref, kv_send.at[n], kv_recv.at[n], (c, h)).wait_recv()
            go(remote(ref, ref, pair_send.at[n], pair_recv.at[n], (sib, h)))

    qrow = iota((256, 512), 0)
    kcol = iota((256, 512), 1)

    def summary_tile(i):
        rows = pl.ds(pl.multiple_of(i * 256, 256), 256)
        qs = q[rows, :]
        own_rows = pl.ds(pl.multiple_of(WINDOW + i * 256, 256), 256)
        ks = kv[0, own_rows, :].astype(F32)
        vs = kv[1, own_rows, :].astype(F32)
        self_score = jnp.sum(qs.astype(F32) * ks, axis=-1, keepdims=True)
        apart = (iota((256, 1), 0) & 127) < 120
        state = (
            jnp.where(apart, self_score, NEG),
            jnp.where(apart, 1.0, 0.0),
            jnp.where(apart, vs, 0.0),
        )

        def step(t, state):
            return fold(
                qs, summ[0, t].reshape(512, HEAD_SIZE), summ[1, t].reshape(512, HEAD_SIZE), state
            )

        state = lax.fori_loop(0, zh, step, state)
        at = qrow + (i * 256 + (2 * x + core) * TOKENS)
        key_at = (kcol >> 3) * 128 + 120 + (kcol & 7)
        state = fold(
            qs, summ[0, zh].reshape(512, HEAD_SIZE), summ[1, zh].reshape(512, HEAD_SIZE),
            state, key_at <= at,
        )
        ls[rows, :] = ls[rows, :] + state[2] / state[1]

    @pl.loop(0, 2)
    def _(i):
        summary_tile(i)

    w_relay(0)
    take_pairs(range(0, 8))

    @pl.loop(2, 4)
    def _(i):
        summary_tile(i)

    w_relay(1)
    take_pairs(range(8, 15))
    own[0].wait()
    own[1].wait()
    for n in range(15):
        dz, dx = offs[n]
        src = ((zh - dz + 4) % 4) * 4 + (x - dx + 4) % 4
        remote(rq.at[src], rq.at[src], q_send.at[n], q_recv.at[n], (c, h)).wait_recv()
        ref = rkv.at[:, src, 1 - core]
        remote(ref, ref, pair_send.at[n], pair_recv.at[n], (sib, h)).wait_recv()
    ref = rkv.at[:, chip, 1 - core]
    remote(ref, ref, pair_send.at[15], pair_recv.at[15], (sib, h)).wait_recv()

    nrow = iota((256, 512), 0)
    order = (nrow >> 6) * 128 + core * 64 + (nrow & 63)

    def stride_tile(n, dz):
        b = (zh + dz) % 4
        qs = rq[pl.ds(b * 4, 4)].reshape(256, HEAD_SIZE)

        def keys(t):
            return (
                rkv[0, pl.ds(t * 4, 4)].reshape(512, HEAD_SIZE),
                rkv[1, pl.ds(t * 4, 4)].reshape(512, HEAD_SIZE),
            )

        def step(t, state):
            return fold(qs, *keys(t), state)

        state = (
            jnp.full((256, 1), NEG, F32), jnp.zeros((256, 1), F32),
            jnp.zeros((256, HEAD_SIZE), F32),
        )
        state = lax.fori_loop(0, b, step, state)
        state = fold(qs, *keys(b), state, kcol <= order)
        ret_out[n] = (state[2] / state[1]).astype(BF16).reshape(4, ROWS, HEAD_SIZE)

    back = [(n, dz, dx) for n, dz in enumerate((2, 1, 3, 0)) for dx in (2, 1, 3, 0)]

    def send_back(n, dz):
        for m, (nn, _, dx) in enumerate(back):
            if nn != n or not (dz or dx):
                continue
            to = chip_at(dz, dx)
            go(remote(
                ret_out.at[n, (x + dx) % 4], ret.at[chip], r_send.at[m], r_recv.at[m],
                (to * 2 + core, h),
            ))

    for n, dz in enumerate((2, 1, 3, 0)):
        stride_tile(n, dz)
        send_back(n, dz)
        if n == 1:
            w_relay(2)
    mine = pltpu.make_async_copy(ret_out.at[3, x], ret.at[chip], in_sem.at[7])
    mine.start()
    w_relay(3)
    mine.wait()
    for m, (n, dz, dx) in enumerate(back):
        if dz or dx:
            src = ((zh - dz + 4) % 4) * 4 + (x - dx + 4) % 4
            remote(ret.at[src], ret.at[src], r_send.at[m], r_recv.at[m], (c, h)).wait_recv()
    for b in range(4):
        rows = ret[:, pl.ds(16 * b, 16), :].reshape(256, HEAD_SIZE)
        back_rows = jnp.dot(swap, rows, preferred_element_type=F32)
        att_out[pl.ds(256 * b, 256), :] = (ls[pl.ds(256 * b, 256), :] + back_rows).astype(BF16)
    for n, (dy, dz) in enumerate(heads):
        to = ((y + dy) % 8) * 2 + (zl + dz) % 2
        go(remote(
            att_out.at[pl.ds(pl.multiple_of(to * 64, 64), 64)], att.at[h],
            a_send.at[n], a_recv.at[n], (c, to),
        ))
    mine = pltpu.make_async_copy(
        att_out.at[pl.ds(pl.multiple_of(h * 64, 64), 64)], att.at[h], in_sem.at[8]
    )
    mine.start()
    w_relay(4)
    w_relay(5)
    w_relay(6)
    mine.wait()
    for n, (dy, dz) in enumerate(heads):
        src = ((y - dy + 8) % 8) * 2 + (zl + dz) % 2
        remote(att.at[src], att.at[src], a_send.at[n], a_recv.at[n], (c, h)).wait_recv()
    ref = w_unit(y, 1 - zl, 1 - core)
    remote(ref, ref, wp_send.at[0], wp_recv.at[0], (sib, h)).wait_recv()
    for d in range(2):
        for i in range(7):
            yy, zz = w_name(d, i)
            ref = w_unit(yy - (1, -1)[d] + 8, zz, 1 - core)
            n = 1 + 7 * d + i
            remote(ref, ref, wp_send.at[n], wp_recv.at[n], (sib, h)).wait_recv()

    rows = jnp.concatenate([att[i] for i in range(16)], axis=-1)

    @pl.loop(0, 4)
    def _(n):
        cols = pl.ds(pl.multiple_of(n * 512, 512), 512)
        weights = wbuf[:, :, cols].reshape(2048, 512)
        out_ref[:, cols] = jnp.dot(rows, weights, preferred_element_type=F32).astype(BF16)

    for copy in sends:
        copy.wait_send()


def body(queries, keys, values, out_weight):
    dma = pltpu.SemaphoreType.DMA
    return pl.pallas_call(
        kernel,
        out_shape=jax.ShapeDtypeStruct((64, 2048), BF16),
        in_specs=[pl.BlockSpec(memory_space=pl.ANY)] * 4,
        out_specs=pl.BlockSpec(memory_space=pltpu.VMEM),
        scratch_shapes=[
            pltpu.VMEM((TOKENS, HEAD_SIZE), BF16),
            pltpu.VMEM((2, WINDOW + TOKENS, HEAD_SIZE), BF16),
            pltpu.VMEM((CHIPS, 3, ROWS, HEAD_SIZE), BF16),
            pltpu.VMEM((CHIPS, ROWS, HEAD_SIZE), BF16),
            pltpu.VMEM((2, CHIPS, 2, ROWS, HEAD_SIZE), BF16),
            pltpu.VMEM((2, ROWS, HEAD_SIZE), BF16),
            pltpu.VMEM((2, 4, 4, 2, ROWS, HEAD_SIZE), BF16),
            pltpu.VMEM((TOKENS, HEAD_SIZE), F32),
            pltpu.VMEM((4, 4, ROWS, HEAD_SIZE), BF16),
            pltpu.VMEM((CHIPS, ROWS, HEAD_SIZE), BF16),
            pltpu.VMEM((TOKENS, HEAD_SIZE), BF16),
            pltpu.VMEM((16, 64, HEAD_SIZE), BF16),
            pltpu.VMEM((16, HEAD_SIZE, 2048), BF16),
            dma((9,)), pltpu.SemaphoreType.REGULAR, dma((2,)),
            dma((15,)), dma((15,)), dma((15,)), dma((15,)), dma((16,)), dma((16,)),
            dma((3,)), dma((3,)), dma((3,)), dma((3,)), dma((4,)), dma((4,)),
            dma((2,)), dma((2, 7)), dma((2, 7)), dma((15,)), dma((15,)),
            dma((16,)), dma((16,)), dma((15,)), dma((15,)),
        ],
        compiler_params=pltpu.CompilerParams(collective_id=0, has_side_effects=True),
    )(queries, keys, values, out_weight)


def solution(mesh):
    placed = (P("ctx", "head"), P("ctx", "head"), P("ctx", "head"), P("head", None))
    return jax.shard_map(
        body, mesh=mesh, in_specs=placed, out_specs=P(("ctx", "head"), None), check_vma=False
    )
```

```python
import functools
import math

import jax
import jax.numpy as jnp
from jax import lax
from jax.experimental import pallas as pl
from jax.experimental.pallas import tpu as pltpu
from jax.sharding import PartitionSpec as P

MESH = pl.DeviceIdType.MESH
NEG = -1e30
HEAD_SIZE = 128
WINDOW = 512
LOGIT = math.log2(math.e) * HEAD_SIZE ** -0.5
F32 = jnp.float32
BF16 = jnp.bfloat16
TOKENS = 1024
CHIPS = 16
ROWS = 64
LT = 256
SPAN = LT + WINDOW


def scores(q, k):
    return lax.dot_general(q, k, (((1,), (1,)), ((), ())), preferred_element_type=F32)


def mix(p, v):
    return jnp.dot(p.astype(BF16), v, preferred_element_type=F32)


def fold(q, k, v, state, allowed=None):
    top, total, acc = state
    s = scores(q, k)
    if allowed is not None:
        s = jnp.where(allowed, s, NEG)
    new_top = jnp.maximum(top, jnp.max(s, axis=-1, keepdims=True))
    p = jnp.exp2((s - new_top) * LOGIT)
    shrink = jnp.exp2((top - new_top) * LOGIT)
    total = shrink * total + jnp.sum(p, axis=-1, keepdims=True)
    acc = shrink * acc + mix(p, v)
    return new_top, total, acc


def iota(shape, dim):
    return lax.broadcasted_iota(jnp.int32, shape, dim)


SHIFTS = (2, 1, 3, 0)
PART = 32


def kernel(
    q_hbm, k_hbm, v_hbm, w_hbm, out_ref,
    q, kv, stage_q, stage_kv, rq, rkv, own_sum, summ, near, far, ret_out, ret, att_out, att, wbuf,
    in_sem, halo_sem, q_send, q_recv, kv_send, kv_recv, pair_send, pair_recv,
    sz_send, sz_recv, sx_send, sx_recv, sp_send, sp_recv,
    wz_send, wz_recv, wy_send, wy_recv, wx_send, wx_recv, wp_send, wp_recv,
    r_send, r_recv, own_sem, a_send, a_recv,
):
    c = lax.axis_index("ctx")
    h = lax.axis_index("head")
    core, x, zh = c % 2, (c // 2) % 4, c // 8
    zl, y = h % 2, h // 2
    chip = zh * 4 + x
    sib = (c + 1 - 2 * core, h)
    sends = []

    def remote(src, dst, ssem, rsem, dev):
        return pltpu.make_async_remote_copy(
            src_ref=src, dst_ref=dst, send_sem=ssem, recv_sem=rsem,
            device_id=dev, device_id_type=MESH,
        )

    def go(src, dst, ssem, rsem, dev):
        copy = remote(src, dst, ssem, rsem, dev)
        copy.start()
        sends.append(copy)

    def got(ref, sem):
        remote(ref, ref, sem, sem, sib).wait_recv()

    def chip_at(dz, dx):
        return ((zh + dz) % 4) * 4 + (x + dx) % 4

    def source(dz, dx):
        return ((zh - dz + 4) % 4) * 4 + (x - dx + 4) % 4

    def block(i):
        return (y // 2 + SHIFTS[i]) % 4

    offs = [(dz, dx) for dz in (2, 1, 3, 0) for dx in (2, 1, 3, 0) if dz or dx]
    quads = [(a, b) for a in range(2) for b in range(2)]

    loads = [
        pltpu.make_async_copy(q_hbm, q, in_sem.at[0]),
        pltpu.make_async_copy(k_hbm, kv.at[0, pl.ds(WINDOW, TOKENS)], in_sem.at[1]),
        pltpu.make_async_copy(v_hbm, kv.at[1, pl.ds(WINDOW, TOKENS)], in_sem.at[2]),
        pltpu.make_async_copy(w_hbm, wbuf.at[h], in_sem.at[3]),
    ]
    for load in loads:
        load.start()

    barrier = pltpu.get_barrier_semaphore()

    def greet(dev):
        pl.semaphore_signal(barrier, inc=1, device_id=dev, device_id_type=MESH)

    zfar = (((zh + 2 * zl - 1 + 4) % 4) * 8 + x * 2 + core, 2 * y + 1 - zl)
    zpeer = (c, 2 * y + 1 - zl)
    for dz, dx in offs:
        greet((chip_at(dz, dx) * 2 + core, h))
    for dy in (4, 3, 5, 2, 6, 1, 7, 0):
        for dz in (1, 0):
            if dy or dz:
                greet((c, ((y + dy) % 8) * 2 + (zl + dz) % 2))
    greet(((c + 2 * core - 1) % 32, h))
    greet(zfar)
    greet(sib)

    for load in loads[:3]:
        load.wait()

    ri, ci = iota((256, 256), 0), iota((256, 256), 1)
    swap = jnp.where(((ri >> 4) == (ci & 15)) & ((ri & 15) == (ci >> 4)), 1.0, 0.0).astype(BF16)
    for n in range(2):
        parts = [
            kv[n, pl.ds(WINDOW + 128 * g + 112, 16), :].astype(F32)[8:] for g in range(8)
        ]
        own_sum[n] = jnp.concatenate(parts, axis=0).astype(BF16)
        for b in range(4):
            rows = kv[n, pl.ds(WINDOW + 256 * b, 256), :]
            moved = jnp.dot(swap, rows, preferred_element_type=F32).astype(BF16)
            stage_kv[:, n, pl.ds(16 * b, 16), :] = moved.reshape(CHIPS, 16, HEAD_SIZE)
    for i in range(4):
        rows = q[pl.ds(pl.multiple_of(256 * block(i), 256), 256), :]
        moved = jnp.dot(swap, rows, preferred_element_type=F32).astype(BF16)
        stage_q[i] = moved.reshape(CHIPS, 16, HEAD_SIZE)

    rr, cc = iota((LT, SPAN), 0), iota((LT, SPAN), 1)

    def local_tile(i, bias):
        rows = pl.ds(pl.multiple_of(i * LT, LT), LT)
        window = pl.ds(pl.multiple_of(i * LT, LT), SPAN)
        s = scores(q[rows, :], kv[0, window, :])
        allowed = (cc > rr) & (cc <= rr + WINDOW)
        if bias:
            start = jnp.where(c == 0, WINDOW - i * LT, 0)
            allowed = allowed & (cc >= start)
        s = jnp.where(allowed, s, NEG)
        top = jnp.max(s, axis=-1, keepdims=True)
        p = jnp.exp2((s - top) * LOGIT)
        total = jnp.sum(p, axis=-1, keepdims=True)
        near[rows, :] = mix(p, kv[1, window, :]) / total

    half = WINDOW // LT

    @pl.loop(half, TOKENS // LT)
    def _(i):
        local_tile(i, False)

    pl.semaphore_wait(barrier, 33)

    STEP = (1, 7)
    side = x % 2
    xnext = (zh * 8 + (x + 1 - 2 * side) * 2 + core, h)

    def w_piece(yy, kind, k, p):
        zz = zl if kind == 0 else 1 - zl
        start = pl.multiple_of(64 * k + PART * ((side + p) % 2), PART)
        return wbuf.at[2 * (yy % 8) + zz, pl.ds(start, PART), :]

    orders = [
        [
            (kind, s, p)
            for kind in range(2)
            for s in range(4 - (kind != d))
            for p in range(2 if s < 2 else 1)
        ]
        for d in range(2)
    ]
    place = [{key: n for n, key in enumerate(orders[d])} for d in range(2)]
    distant = [(d, key) for d in range(2) for key in orders[d] if key[1] >= 2]
    w_count = len(orders[0])

    def w_send(d, key):
        kind, s, p = key
        ref = w_piece(y + (8 - STEP[d]) * s, kind, core, p)
        n = place[d][key]
        go(ref, ref, wy_send.at[d, n], wy_recv.at[d, n], (c, 2 * ((y + STEP[d]) % 8) + zl))

    def w_pair(ref, n):
        go(ref, ref, wp_send.at[n], wp_recv.at[n], sib)

    def w_got(d, key, k, other=0):
        kind, s, p = key
        return w_piece(y + (8 - STEP[d]) * (s + 1), kind, k, p + other)

    def w_relay(*numbers):
        for n in numbers:
            for d in range(2):
                key = orders[d][n]
                kind, s, p = key
                ref = w_got(d, key, core)
                got(ref, wy_recv.at[d, n])
                if (kind, s + 1, p) in place[d]:
                    w_send(d, (kind, s + 1, p))
                if s >= 2:
                    m = distant.index((d, key))
                    go(ref, ref, wx_send.at[m], wx_recv.at[m], xnext)
                w_pair(ref, 2 + w_count * d + n)

    def w_cross(*numbers):
        for m in numbers:
            ref = w_got(*distant[m], core, 1)
            got(ref, wx_recv.at[m])
            w_pair(ref, 2 + 2 * w_count + m)

    def w_swap():
        for p, dev in enumerate((zpeer, zfar)):
            start = pl.multiple_of(64 * core + PART * p, PART)
            ref = wbuf.at[h, pl.ds(start, PART), :]
            go(ref, ref, wz_send.at[p], wz_recv.at[p], dev)

    def w_other_part(p, k):
        return wbuf.at[2 * y + 1 - zl, pl.ds(pl.multiple_of(64 * k + PART * p, PART), PART), :]

    def w_other():
        for p in range(2):
            ref = w_other_part(p, core)
            got(ref, wz_recv.at[p])
            w_pair(ref, p)
        for p in range(2):
            w_send(0, (1, 0, p))
            w_send(1, (1, 0, p))

    def w_finish():
        for p in range(2):
            got(w_other_part(p, 1 - core), wp_recv.at[p])
        for d in range(2):
            for n, key in enumerate(orders[d]):
                got(w_got(d, key, 1 - core), wp_recv.at[2 + w_count * d + n])
        for m, (d, key) in enumerate(distant):
            got(w_got(d, key, 1 - core, 1), wp_recv.at[2 + 2 * w_count + m])

    for n, dz in enumerate((2, 1, 3)):
        dev = (((zh + dz) % 4) * 8 + x * 2 + core, h)
        go(own_sum, summ.at[:, zh, x, core], sz_send.at[n], sz_recv.at[n], dev)
    loads[3].wait()
    for p in range(2):
        w_send(0, (0, 0, p))
        w_send(1, (0, 0, p))
    for n, (dz, dx) in enumerate(offs):
        to = chip_at(dz, dx)
        go(stage_kv.at[to], rkv.at[:, chip, core], kv_send.at[n], kv_recv.at[n], (to * 2 + core, h))
    w_swap()
    for i in range(4):
        for n, (dz, dx) in enumerate(offs):
            to = chip_at(dz, dx)
            go(stage_q.at[i, to], rq.at[i, chip], q_send.at[i, n], q_recv.at[i, n], (to * 2 + core, h))
    halo_to = kv.at[:, pl.ds(0, WINDOW)]
    go(kv.at[:, pl.ds(TOKENS, WINDOW)], halo_to, halo_sem.at[0], halo_sem.at[1], ((c + 1) % 32, h))
    own = [
        pltpu.make_async_copy(stage_kv.at[chip], rkv.at[:, chip, core], in_sem.at[4]),
        pltpu.make_async_copy(stage_q.at[:, chip], rq.at[:, chip], in_sem.at[5]),
        pltpu.make_async_copy(own_sum, summ.at[:, zh, x, core], in_sem.at[6]),
    ]
    for copy in own:
        copy.start()
    go(stage_kv.at[chip], rkv.at[:, chip, core], pair_send.at[15], pair_recv.at[15], sib)

    def take_pairs(numbers):
        for n in numbers:
            ref = rkv.at[:, source(*offs[n]), core]
            got(ref, kv_recv.at[n])
            go(ref, ref, pair_send.at[n], pair_recv.at[n], sib)

    qrow = iota((256, 512), 0)
    kcol = iota((256, 512), 1)

    def summary_tile(i):
        b = block(i)
        rows = pl.ds(pl.multiple_of(b * 256, 256), 256)
        qs = q[rows, :]
        own_rows = pl.ds(pl.multiple_of(WINDOW + b * 256, 256), 256)
        ks = kv[0, own_rows, :].astype(F32)
        vs = kv[1, own_rows, :].astype(F32)
        self_score = jnp.sum(qs.astype(F32) * ks, axis=-1, keepdims=True)
        apart = (iota((256, 1), 0) & 127) < 120
        state = (
            jnp.where(apart, self_score, NEG),
            jnp.where(apart, 1.0, 0.0),
            jnp.where(apart, vs, 0.0),
        )

        def step(t, state):
            return fold(
                qs, summ[0, t].reshape(512, HEAD_SIZE), summ[1, t].reshape(512, HEAD_SIZE), state
            )

        state = lax.fori_loop(0, zh, step, state)
        at = qrow + (b * 256 + (2 * x + core) * TOKENS)
        key_at = (kcol >> 3) * 128 + 120 + (kcol & 7)
        state = fold(
            qs, summ[0, zh].reshape(512, HEAD_SIZE), summ[1, zh].reshape(512, HEAD_SIZE),
            state, key_at <= at,
        )
        far[rows, :] = state[2] / state[1]

    def summary_spread():
        own[2].wait()
        for n, dz in enumerate((2, 1, 3)):
            got(summ.at[:, (zh - dz + 4) % 4, x, core], sz_recv.at[n])
        ref = summ.at[:, :, x, core]
        for n, dx in enumerate((2, 1, 3)):
            dev = (zh * 8 + ((x + dx) % 4) * 2 + core, h)
            go(ref, ref, sx_send.at[n], sx_recv.at[n], dev)
        go(ref, ref, sp_send.at[3], sp_recv.at[3], sib)

    def summary_pair():
        for n, dx in enumerate((2, 1, 3)):
            ref = summ.at[:, :, (x - dx + 4) % 4, core]
            got(ref, sx_recv.at[n])
            go(ref, ref, sp_send.at[n], sp_recv.at[n], sib)

    def summary_ready():
        for n, dx in enumerate((2, 1, 3, 0)):
            got(summ.at[:, :, (x - dx + 4) % 4, 1 - core], sp_recv.at[n])

    def strided_ready():
        own[0].wait()
        own[1].wait()
        for n in range(15):
            got(rkv.at[:, source(*offs[n]), 1 - core], pair_recv.at[n])
        got(rkv.at[:, chip, 1 - core], pair_recv.at[15])

    drow, dcol = iota((64, 512), 0), iota((64, 512), 1)

    def stride_block(i):
        for n in range(15):
            got(rq.at[i, source(*offs[n])], q_recv.at[i, n])
        qs = rq[i].reshape(256, HEAD_SIZE)
        allowed = dcol <= (drow >> 4) * 128 + (drow & 15) + (core * 64 + block(i) * 16)
        state = None
        for t in range(4):
            ks = rkv[0, pl.ds(t * 4, 4)].reshape(512, HEAD_SIZE)
            vs = rkv[1, pl.ds(t * 4, 4)].reshape(512, HEAD_SIZE)
            s = scores(qs[64 * t :], ks)
            first = jnp.where(allowed, s[:64], NEG)
            s = first if t == 3 else jnp.concatenate([first, s[64:]], axis=0)
            top = jnp.max(s, axis=-1, keepdims=True)
            if t:
                top = jnp.maximum(top, state[0])
            p = jnp.exp2((s - top) * LOGIT)
            total = jnp.sum(p, axis=-1, keepdims=True)
            acc = mix(p, vs)
            if t:
                shrink = jnp.exp2((state[0] - top) * LOGIT)
                total = total + shrink * state[1]
                acc = acc + shrink * state[2]
            done = (acc[:64] / total[:64]).astype(BF16)
            ret_out[i, pl.ds(4 * t, 4)] = done.reshape(4, 16, HEAD_SIZE)
            if t < 3:
                state = (top[64:], total[64:], acc[64:])
        for n, (dz, dx) in enumerate(offs):
            to = chip_at(dz, dx)
            go(ret_out.at[i, to], ret.at[i, chip], r_send.at[i, n], r_recv.at[i, n], (to * 2 + core, h))
        pltpu.make_async_copy(ret_out.at[i, chip], ret.at[i, chip], own_sem.at[i]).start()

    def join_block(i):
        pltpu.make_async_copy(ret_out.at[i, chip], ret.at[i, chip], own_sem.at[i]).wait()
        for n in range(15):
            got(ret.at[i, source(*offs[n])], r_recv.at[i, n])
        rows = pl.ds(pl.multiple_of(block(i) * 256, 256), 256)
        strided = jnp.dot(swap, ret[i].reshape(256, HEAD_SIZE), preferred_element_type=F32)
        att_out[i] = (near[rows, :] + far[rows, :] + strided).astype(BF16)
        for m, (dy, dz) in enumerate(quads):
            yy, zz = (y + dy) % 2, (zl + dz) % 2
            part = att_out.at[i, pl.ds(pl.multiple_of(64 * (2 * yy + zz), 64), 64)]
            if SHIFTS[i] or dy or dz:
                dev = (c, 4 * block(i) + 2 * yy + zz)
                go(part, att.at[h], a_send.at[i, m], a_recv.at[i, m], dev)
            else:
                pltpu.make_async_copy(part, att.at[h], own_sem.at[4]).start()

    def attended_ready():
        for i in range(4):
            for m, (dy, dz) in enumerate(quads):
                src = 4 * ((y // 2 - SHIFTS[i] + 4) % 4) + 2 * ((y + dy) % 2) + (zl + dz) % 2
                if SHIFTS[i] or dy or dz:
                    got(att.at[src], a_recv.at[i, m])
                else:
                    pltpu.make_async_copy(att.at[src], att.at[src], own_sem.at[4]).wait()

    w_relay(0)
    summary_spread()
    w_relay(1, 2)
    take_pairs(range(0, 5))
    w_relay(3)
    summary_pair()
    take_pairs(range(5, 15))
    w_relay(4)
    summary_ready()
    summary_tile(0)
    w_other()
    summary_tile(1)
    w_relay(5)
    strided_ready()
    stride_block(0)
    stride_block(1)
    w_relay(6)
    stride_block(2)
    stride_block(3)
    w_relay(7)
    got(halo_to, halo_sem.at[1])

    @pl.loop(0, half)
    def _(i):
        local_tile(i, True)

    join_block(0)
    w_relay(8)
    summary_tile(2)
    join_block(1)
    summary_tile(3)
    w_relay(9)
    join_block(2)
    join_block(3)
    w_cross(0, 1, 3)
    w_relay(10)
    w_cross(2, 4, 5)
    attended_ready()
    w_finish()

    rows = jnp.concatenate([att[i] for i in range(16)], axis=-1)

    @pl.loop(0, 4)
    def _(n):
        cols = pl.ds(pl.multiple_of(n * 512, 512), 512)
        weights = wbuf[:, :, cols].reshape(2048, 512)
        out_ref[:, cols] = jnp.dot(rows, weights, preferred_element_type=F32).astype(BF16)

    for copy in sends:
        copy.wait_send()


def body(queries, keys, values, out_weight):
    dma = pltpu.SemaphoreType.DMA
    wide = (CHIPS, 16, HEAD_SIZE)
    return pl.pallas_call(
        kernel,
        out_shape=jax.ShapeDtypeStruct((64, 2048), BF16),
        in_specs=[pl.BlockSpec(memory_space=pl.ANY)] * 4,
        out_specs=pl.BlockSpec(memory_space=pltpu.VMEM),
        scratch_shapes=[
            pltpu.VMEM((TOKENS, HEAD_SIZE), BF16),
            pltpu.VMEM((2, WINDOW + TOKENS, HEAD_SIZE), BF16),
            pltpu.VMEM((4, *wide), BF16),
            pltpu.VMEM((CHIPS, 2, ROWS, HEAD_SIZE), BF16),
            pltpu.VMEM((4, *wide), BF16),
            pltpu.VMEM((2, CHIPS, 2, ROWS, HEAD_SIZE), BF16),
            pltpu.VMEM((2, ROWS, HEAD_SIZE), BF16),
            pltpu.VMEM((2, 4, 4, 2, ROWS, HEAD_SIZE), BF16),
            pltpu.VMEM((TOKENS, HEAD_SIZE), F32),
            pltpu.VMEM((TOKENS, HEAD_SIZE), F32),
            pltpu.VMEM((4, *wide), BF16),
            pltpu.VMEM((4, *wide), BF16),
            pltpu.VMEM((4, 256, HEAD_SIZE), BF16),
            pltpu.VMEM((16, 64, HEAD_SIZE), BF16),
            pltpu.VMEM((16, HEAD_SIZE, 2048), BF16),
            dma((7,)), dma((2,)), dma((4, 15)), dma((4, 15)), dma((15,)), dma((15,)),
            dma((16,)), dma((16,)),
            dma((3,)), dma((3,)), dma((3,)), dma((3,)), dma((4,)), dma((4,)),
            dma((2,)), dma((2,)), dma((2, 11)), dma((2, 11)), dma((6,)), dma((6,)),
            dma((30,)), dma((30,)),
            dma((4, 15)), dma((4, 15)), dma((5,)), dma((4, 4)), dma((4, 4)),
        ],
        compiler_params=pltpu.CompilerParams(collective_id=0, has_side_effects=True),
    )(queries, keys, values, out_weight)


def solution(mesh):
    placed = (P("ctx", "head"), P("ctx", "head"), P("ctx", "head"), P("head", None))
    return jax.shard_map(
        body, mesh=mesh, in_specs=placed, out_specs=P(("ctx", "head"), None), check_vma=False
    )
```

```python
import functools
import math

import jax
import jax.numpy as jnp
from jax import lax
from jax.experimental import pallas as pl
from jax.experimental.pallas import tpu as pltpu
from jax.sharding import PartitionSpec as P

MESH = pl.DeviceIdType.MESH
NEG = -1e30
HEAD_SIZE = 128
WINDOW = 512
LOGIT = math.log2(math.e) * HEAD_SIZE ** -0.5
F32 = jnp.float32
BF16 = jnp.bfloat16
TOKENS = 1024
CHIPS = 16
ROWS = 64
LT = 256
SPAN = LT + WINDOW


def scores(q, k):
    return lax.dot_general(q, k, (((1,), (1,)), ((), ())), preferred_element_type=F32)


def mix(p, v):
    return jnp.dot(p.astype(BF16), v, preferred_element_type=F32)


def fold(q, k, v, state, allowed=None):
    top, total, acc = state
    s = scores(q, k)
    if allowed is not None:
        s = jnp.where(allowed, s, NEG)
    new_top = jnp.maximum(top, jnp.max(s, axis=-1, keepdims=True))
    p = jnp.exp2((s - new_top) * LOGIT)
    shrink = jnp.exp2((top - new_top) * LOGIT)
    total = shrink * total + jnp.sum(p, axis=-1, keepdims=True)
    acc = shrink * acc + mix(p, v)
    return new_top, total, acc


def iota(shape, dim):
    return lax.broadcasted_iota(jnp.int32, shape, dim)


SHIFTS = (2, 1, 3, 0)
PART = 32


def kernel(
    q_hbm, k_hbm, v_hbm, w_hbm, out_ref,
    q, kv, stage_q, stage_kv, rq, rkv, own_sum, summ, near, far, ret_out, ret, att_out, att, wbuf,
    in_sem, halo_sem, q_send, q_recv, kv_send, kv_recv, pair_send, pair_recv,
    sz_send, sz_recv, sx_send, sx_recv, sp_send, sp_recv,
    wz_send, wz_recv, wy_send, wy_recv, wx_send, wx_recv, wp_send, wp_recv,
    r_send, r_recv, own_sem, a_send, a_recv,
):
    c = lax.axis_index("ctx")
    h = lax.axis_index("head")
    core, x, zh = c % 2, (c // 2) % 4, c // 8
    zl, y = h % 2, h // 2
    chip = zh * 4 + x
    sib = (c + 1 - 2 * core, h)
    sends = []

    def remote(src, dst, ssem, rsem, dev):
        return pltpu.make_async_remote_copy(
            src_ref=src, dst_ref=dst, send_sem=ssem, recv_sem=rsem,
            device_id=dev, device_id_type=MESH,
        )

    def go(src, dst, ssem, rsem, dev):
        copy = remote(src, dst, ssem, rsem, dev)
        copy.start()
        sends.append(copy)

    def got(ref, sem):
        remote(ref, ref, sem, sem, sib).wait_recv()

    def chip_at(dz, dx):
        return ((zh + dz) % 4) * 4 + (x + dx) % 4

    def source(dz, dx):
        return ((zh - dz + 4) % 4) * 4 + (x - dx + 4) % 4

    def block(i):
        return (y // 2 + SHIFTS[i]) % 4

    offs = [(dz, dx) for dz in (2, 1, 3, 0) for dx in (2, 1, 3, 0) if dz or dx]
    quads = [(a, b) for a in range(2) for b in range(2)]

    loads = [
        pltpu.make_async_copy(q_hbm, q, in_sem.at[0]),
        pltpu.make_async_copy(k_hbm, kv.at[0, pl.ds(WINDOW, TOKENS)], in_sem.at[1]),
        pltpu.make_async_copy(v_hbm, kv.at[1, pl.ds(WINDOW, TOKENS)], in_sem.at[2]),
        pltpu.make_async_copy(w_hbm, wbuf.at[h], in_sem.at[3]),
    ]
    for load in loads:
        load.start()

    barrier = pltpu.get_barrier_semaphore()

    def greet(dev):
        pl.semaphore_signal(barrier, inc=1, device_id=dev, device_id_type=MESH)

    zfar = (((zh + 2 * zl - 1 + 4) % 4) * 8 + x * 2 + core, 2 * y + 1 - zl)
    zpeer = (c, 2 * y + 1 - zl)
    for dz, dx in offs:
        greet((chip_at(dz, dx) * 2 + core, h))
    for dy in (4, 3, 5, 2, 6, 1, 7, 0):
        for dz in (1, 0):
            if dy or dz:
                greet((c, ((y + dy) % 8) * 2 + (zl + dz) % 2))
    greet(((c + 2 * core - 1) % 32, h))
    greet(zfar)
    greet(sib)

    for load in loads[:3]:
        load.wait()

    ri, ci = iota((256, 256), 0), iota((256, 256), 1)
    swap = jnp.where(((ri >> 4) == (ci & 15)) & ((ri & 15) == (ci >> 4)), 1.0, 0.0).astype(BF16)
    for n in range(2):
        parts = [
            kv[n, pl.ds(WINDOW + 128 * g + 112, 16), :].astype(F32)[8:] for g in range(8)
        ]
        own_sum[n] = jnp.concatenate(parts, axis=0).astype(BF16)
        for b in range(4):
            rows = kv[n, pl.ds(WINDOW + 256 * b, 256), :]
            moved = jnp.dot(swap, rows, preferred_element_type=F32).astype(BF16)
            stage_kv[:, n, pl.ds(16 * b, 16), :] = moved.reshape(CHIPS, 16, HEAD_SIZE)
    for i in range(4):
        rows = q[pl.ds(pl.multiple_of(256 * block(i), 256), 256), :]
        moved = jnp.dot(swap, rows, preferred_element_type=F32).astype(BF16)
        stage_q[i] = moved.reshape(CHIPS, 16, HEAD_SIZE)

    rr, cc = iota((LT, SPAN), 0), iota((LT, SPAN), 1)

    def local_tile(i, bias):
        rows = pl.ds(pl.multiple_of(i * LT, LT), LT)
        window = pl.ds(pl.multiple_of(i * LT, LT), SPAN)
        s = scores(q[rows, :], kv[0, window, :])
        allowed = (cc > rr) & (cc <= rr + WINDOW)
        if bias:
            start = jnp.where(c == 0, WINDOW - i * LT, 0)
            allowed = allowed & (cc >= start)
        s = jnp.where(allowed, s, NEG)
        top = jnp.max(s, axis=-1, keepdims=True)
        p = jnp.exp2((s - top) * LOGIT)
        total = jnp.sum(p, axis=-1, keepdims=True)
        near[rows, :] = mix(p, kv[1, window, :]) / total

    half = WINDOW // LT

    @pl.loop(half, TOKENS // LT)
    def _(i):
        local_tile(i, False)

    pl.semaphore_wait(barrier, 33)

    STEP = (1, 7)
    side = x % 2
    xnext = (zh * 8 + (x + 1 - 2 * side) * 2 + core, h)

    def w_piece(yy, kind, k, p):
        zz = zl if kind == 0 else 1 - zl
        start = pl.multiple_of(64 * k + PART * ((side + p) % 2), PART)
        return wbuf.at[2 * (yy % 8) + zz, pl.ds(start, PART), :]

    orders = [
        [
            (kind, s, p)
            for s in range(4)
            for kind in range(2)
            for p in range(2 if s < 2 else 1)
            if s < 3 or kind == d
        ]
        for d in range(2)
    ]
    place = [{key: n for n, key in enumerate(orders[d])} for d in range(2)]
    distant = [(d, key) for d in range(2) for key in orders[d] if key[1] >= 2]
    w_count = len(orders[0])

    def w_send(d, key):
        kind, s, p = key
        ref = w_piece(y + (8 - STEP[d]) * s, kind, core, p)
        n = place[d][key]
        go(ref, ref, wy_send.at[d, n], wy_recv.at[d, n], (c, 2 * ((y + STEP[d]) % 8) + zl))

    def w_pair(ref, n):
        go(ref, ref, wp_send.at[n], wp_recv.at[n], sib)

    def w_got(d, key, k, other=0):
        kind, s, p = key
        return w_piece(y + (8 - STEP[d]) * (s + 1), kind, k, p + other)

    def w_relay(*numbers):
        for n in numbers:
            for d in range(2):
                key = orders[d][n]
                kind, s, p = key
                ref = w_got(d, key, core)
                got(ref, wy_recv.at[d, n])
                if (kind, s + 1, p) in place[d]:
                    w_send(d, (kind, s + 1, p))
                if s >= 2:
                    m = distant.index((d, key))
                    go(ref, ref, wx_send.at[m], wx_recv.at[m], xnext)
                w_pair(ref, 2 + w_count * d + n)

    def w_cross(*numbers):
        for m in numbers:
            ref = w_got(*distant[m], core, 1)
            got(ref, wx_recv.at[m])
            w_pair(ref, 2 + 2 * w_count + m)

    def w_swap():
        for p, dev in enumerate((zpeer, zfar)):
            start = pl.multiple_of(64 * core + PART * p, PART)
            ref = wbuf.at[h, pl.ds(start, PART), :]
            go(ref, ref, wz_send.at[p], wz_recv.at[p], dev)

    def w_other_part(p, k):
        return wbuf.at[2 * y + 1 - zl, pl.ds(pl.multiple_of(64 * k + PART * p, PART), PART), :]

    def w_other():
        for p in range(2):
            ref = w_other_part(p, core)
            got(ref, wz_recv.at[p])
            w_pair(ref, p)
        for p in range(2):
            w_send(0, (1, 0, p))
            w_send(1, (1, 0, p))

    def w_finish():
        for p in range(2):
            got(w_other_part(p, 1 - core), wp_recv.at[p])
        for d in range(2):
            for n, key in enumerate(orders[d]):
                got(w_got(d, key, 1 - core), wp_recv.at[2 + w_count * d + n])
        for m, (d, key) in enumerate(distant):
            got(w_got(d, key, 1 - core, 1), wp_recv.at[2 + 2 * w_count + m])

    loads[3].wait()
    w_swap()
    for p in range(2):
        w_send(0, (0, 0, p))
        w_send(1, (0, 0, p))
    for n, dz in enumerate((2, 1, 3)):
        dev = (((zh + dz) % 4) * 8 + x * 2 + core, h)
        go(own_sum, summ.at[:, zh, x, core], sz_send.at[n], sz_recv.at[n], dev)
    for n, (dz, dx) in enumerate(offs):
        to = chip_at(dz, dx)
        go(stage_kv.at[to], rkv.at[:, chip, core], kv_send.at[n], kv_recv.at[n], (to * 2 + core, h))
    for i in range(4):
        for n, (dz, dx) in enumerate(offs):
            to = chip_at(dz, dx)
            go(stage_q.at[i, to], rq.at[i, chip], q_send.at[i, n], q_recv.at[i, n], (to * 2 + core, h))
    halo_to = kv.at[:, pl.ds(0, WINDOW)]
    go(kv.at[:, pl.ds(TOKENS, WINDOW)], halo_to, halo_sem.at[0], halo_sem.at[1], ((c + 1) % 32, h))
    own = [
        pltpu.make_async_copy(stage_kv.at[chip], rkv.at[:, chip, core], in_sem.at[4]),
        pltpu.make_async_copy(stage_q.at[:, chip], rq.at[:, chip], in_sem.at[5]),
        pltpu.make_async_copy(own_sum, summ.at[:, zh, x, core], in_sem.at[6]),
    ]
    for copy in own:
        copy.start()
    go(stage_kv.at[chip], rkv.at[:, chip, core], pair_send.at[15], pair_recv.at[15], sib)

    def take_pairs(numbers):
        for n in numbers:
            ref = rkv.at[:, source(*offs[n]), core]
            got(ref, kv_recv.at[n])
            go(ref, ref, pair_send.at[n], pair_recv.at[n], sib)

    qrow = iota((256, 512), 0)
    kcol = iota((256, 512), 1)

    def summary_tile(i):
        b = block(i)
        rows = pl.ds(pl.multiple_of(b * 256, 256), 256)
        qs = q[rows, :]
        own_rows = pl.ds(pl.multiple_of(WINDOW + b * 256, 256), 256)
        ks = kv[0, own_rows, :].astype(F32)
        vs = kv[1, own_rows, :].astype(F32)
        self_score = jnp.sum(qs.astype(F32) * ks, axis=-1, keepdims=True)
        apart = (iota((256, 1), 0) & 127) < 120
        state = (
            jnp.where(apart, self_score, NEG),
            jnp.where(apart, 1.0, 0.0),
            jnp.where(apart, vs, 0.0),
        )

        def step(t, state):
            return fold(
                qs, summ[0, t].reshape(512, HEAD_SIZE), summ[1, t].reshape(512, HEAD_SIZE), state
            )

        state = lax.fori_loop(0, zh, step, state)
        at = qrow + (b * 256 + (2 * x + core) * TOKENS)
        key_at = (kcol >> 3) * 128 + 120 + (kcol & 7)
        state = fold(
            qs, summ[0, zh].reshape(512, HEAD_SIZE), summ[1, zh].reshape(512, HEAD_SIZE),
            state, key_at <= at,
        )
        far[rows, :] = state[2] / state[1]

    def summary_spread():
        own[2].wait()
        for n, dz in enumerate((2, 1, 3)):
            got(summ.at[:, (zh - dz + 4) % 4, x, core], sz_recv.at[n])
        ref = summ.at[:, :, x, core]
        for n, dx in enumerate((2, 1, 3)):
            dev = (zh * 8 + ((x + dx) % 4) * 2 + core, h)
            go(ref, ref, sx_send.at[n], sx_recv.at[n], dev)
        go(ref, ref, sp_send.at[3], sp_recv.at[3], sib)

    def summary_pair():
        for n, dx in enumerate((2, 1, 3)):
            ref = summ.at[:, :, (x - dx + 4) % 4, core]
            got(ref, sx_recv.at[n])
            go(ref, ref, sp_send.at[n], sp_recv.at[n], sib)

    def summary_ready():
        for n, dx in enumerate((2, 1, 3, 0)):
            got(summ.at[:, :, (x - dx + 4) % 4, 1 - core], sp_recv.at[n])

    def strided_ready():
        own[0].wait()
        own[1].wait()
        for n in range(15):
            got(rkv.at[:, source(*offs[n]), 1 - core], pair_recv.at[n])
        got(rkv.at[:, chip, 1 - core], pair_recv.at[15])

    drow, dcol = iota((64, 512), 0), iota((64, 512), 1)

    def stride_block(i):
        for n in range(15):
            got(rq.at[i, source(*offs[n])], q_recv.at[i, n])
        qs = rq[i].reshape(256, HEAD_SIZE)
        allowed = dcol <= (drow >> 4) * 128 + (drow & 15) + (core * 64 + block(i) * 16)
        state = None
        for t in range(4):
            ks = rkv[0, pl.ds(t * 4, 4)].reshape(512, HEAD_SIZE)
            vs = rkv[1, pl.ds(t * 4, 4)].reshape(512, HEAD_SIZE)
            s = scores(qs[64 * t :], ks)
            first = jnp.where(allowed, s[:64], NEG)
            s = first if t == 3 else jnp.concatenate([first, s[64:]], axis=0)
            top = jnp.max(s, axis=-1, keepdims=True)
            if t:
                top = jnp.maximum(top, state[0])
            p = jnp.exp2((s - top) * LOGIT)
            total = jnp.sum(p, axis=-1, keepdims=True)
            acc = mix(p, vs)
            if t:
                shrink = jnp.exp2((state[0] - top) * LOGIT)
                total = total + shrink * state[1]
                acc = acc + shrink * state[2]
            done = (acc[:64] / total[:64]).astype(BF16)
            ret_out[i, pl.ds(4 * t, 4)] = done.reshape(4, 16, HEAD_SIZE)
            if t < 3:
                state = (top[64:], total[64:], acc[64:])
        for n, (dz, dx) in enumerate(offs):
            to = chip_at(dz, dx)
            go(ret_out.at[i, to], ret.at[i, chip], r_send.at[i, n], r_recv.at[i, n], (to * 2 + core, h))
        pltpu.make_async_copy(ret_out.at[i, chip], ret.at[i, chip], own_sem.at[i]).start()

    def join_block(i):
        pltpu.make_async_copy(ret_out.at[i, chip], ret.at[i, chip], own_sem.at[i]).wait()
        for n in range(15):
            got(ret.at[i, source(*offs[n])], r_recv.at[i, n])
        rows = pl.ds(pl.multiple_of(block(i) * 256, 256), 256)
        strided = jnp.dot(swap, ret[i].reshape(256, HEAD_SIZE), preferred_element_type=F32)
        att_out[i] = (near[rows, :] + far[rows, :] + strided).astype(BF16)
        for m, (dy, dz) in enumerate(quads):
            yy, zz = (y + dy) % 2, (zl + dz) % 2
            part = att_out.at[i, pl.ds(pl.multiple_of(64 * (2 * yy + zz), 64), 64)]
            if SHIFTS[i] or dy or dz:
                dev = (c, 4 * block(i) + 2 * yy + zz)
                go(part, att.at[h], a_send.at[i, m], a_recv.at[i, m], dev)
            else:
                pltpu.make_async_copy(part, att.at[h], own_sem.at[4]).start()

    def attended_ready():
        for i in range(4):
            for m, (dy, dz) in enumerate(quads):
                src = 4 * ((y // 2 - SHIFTS[i] + 4) % 4) + 2 * ((y + dy) % 2) + (zl + dz) % 2
                if SHIFTS[i] or dy or dz:
                    got(att.at[src], a_recv.at[i, m])
                else:
                    pltpu.make_async_copy(att.at[src], att.at[src], own_sem.at[4]).wait()

    w_other()
    w_relay(0)
    summary_spread()
    w_relay(1, 2)
    summary_pair()
    w_relay(3)
    take_pairs(range(0, 4))
    summary_ready()
    summary_tile(0)
    w_relay(4)
    take_pairs(range(4, 10))
    summary_tile(1)
    w_relay(5)
    take_pairs(range(10, 15))
    summary_tile(2)
    strided_ready()
    stride_block(0)
    stride_block(1)
    w_relay(6)
    stride_block(2)
    stride_block(3)
    w_relay(7)
    summary_tile(3)
    got(halo_to, halo_sem.at[1])

    @pl.loop(0, half)
    def _(i):
        local_tile(i, True)

    join_block(0)
    join_block(1)
    w_relay(8)
    join_block(2)
    join_block(3)
    w_relay(9)
    w_cross(0, 3)
    w_relay(10)
    w_cross(1, 4, 2, 5)
    attended_ready()
    w_finish()

    rows = jnp.concatenate([att[i] for i in range(16)], axis=-1)

    @pl.loop(0, 4)
    def _(n):
        cols = pl.ds(pl.multiple_of(n * 512, 512), 512)
        weights = wbuf[:, :, cols].reshape(2048, 512)
        out_ref[:, cols] = jnp.dot(rows, weights, preferred_element_type=F32).astype(BF16)

    for copy in sends:
        copy.wait_send()


def body(queries, keys, values, out_weight):
    dma = pltpu.SemaphoreType.DMA
    wide = (CHIPS, 16, HEAD_SIZE)
    return pl.pallas_call(
        kernel,
        out_shape=jax.ShapeDtypeStruct((64, 2048), BF16),
        in_specs=[pl.BlockSpec(memory_space=pl.ANY)] * 4,
        out_specs=pl.BlockSpec(memory_space=pltpu.VMEM),
        scratch_shapes=[
            pltpu.VMEM((TOKENS, HEAD_SIZE), BF16),
            pltpu.VMEM((2, WINDOW + TOKENS, HEAD_SIZE), BF16),
            pltpu.VMEM((4, *wide), BF16),
            pltpu.VMEM((CHIPS, 2, ROWS, HEAD_SIZE), BF16),
            pltpu.VMEM((4, *wide), BF16),
            pltpu.VMEM((2, CHIPS, 2, ROWS, HEAD_SIZE), BF16),
            pltpu.VMEM((2, ROWS, HEAD_SIZE), BF16),
            pltpu.VMEM((2, 4, 4, 2, ROWS, HEAD_SIZE), BF16),
            pltpu.VMEM((TOKENS, HEAD_SIZE), F32),
            pltpu.VMEM((TOKENS, HEAD_SIZE), F32),
            pltpu.VMEM((4, *wide), BF16),
            pltpu.VMEM((4, *wide), BF16),
            pltpu.VMEM((4, 256, HEAD_SIZE), BF16),
            pltpu.VMEM((16, 64, HEAD_SIZE), BF16),
            pltpu.VMEM((16, HEAD_SIZE, 2048), BF16),
            dma((7,)), dma((2,)), dma((4, 15)), dma((4, 15)), dma((15,)), dma((15,)),
            dma((16,)), dma((16,)),
            dma((3,)), dma((3,)), dma((3,)), dma((3,)), dma((4,)), dma((4,)),
            dma((2,)), dma((2,)), dma((2, 11)), dma((2, 11)), dma((6,)), dma((6,)),
            dma((30,)), dma((30,)),
            dma((4, 15)), dma((4, 15)), dma((5,)), dma((4, 4)), dma((4, 4)),
        ],
        compiler_params=pltpu.CompilerParams(collective_id=0, has_side_effects=True),
    )(queries, keys, values, out_weight)


def solution(mesh):
    placed = (P("ctx", "head"), P("ctx", "head"), P("ctx", "head"), P("head", None))
    return jax.shard_map(
        body, mesh=mesh, in_specs=placed, out_specs=P(("ctx", "head"), None), check_vma=False
    )
```

```python
import functools
import math

import jax
import jax.numpy as jnp
from jax import lax
from jax.experimental import pallas as pl
from jax.experimental.pallas import tpu as pltpu
from jax.sharding import PartitionSpec as P

MESH = pl.DeviceIdType.MESH
NEG = -1e30
HEAD_SIZE = 128
WINDOW = 512
LOGIT = math.log2(math.e) * HEAD_SIZE ** -0.5
F32 = jnp.float32
BF16 = jnp.bfloat16
TOKENS = 1024
CHIPS = 16
ROWS = 64
LT = 256
SPAN = LT + WINDOW


def scores(q, k):
    return lax.dot_general(q, k, (((1,), (1,)), ((), ())), preferred_element_type=F32)


def mix(p, v):
    return jnp.dot(p.astype(BF16), v, preferred_element_type=F32)


def fold(q, k, v, state, allowed=None):
    top, total, acc = state
    s = scores(q, k)
    if allowed is not None:
        s = jnp.where(allowed, s, NEG)
    new_top = jnp.maximum(top, jnp.max(s, axis=-1, keepdims=True))
    p = jnp.exp2((s - new_top) * LOGIT)
    shrink = jnp.exp2((top - new_top) * LOGIT)
    total = shrink * total + jnp.sum(p, axis=-1, keepdims=True)
    acc = shrink * acc + mix(p, v)
    return new_top, total, acc


def iota(shape, dim):
    return lax.broadcasted_iota(jnp.int32, shape, dim)


SHIFTS = (1, 0)
PART = 32


def kernel(
    q_hbm, k_hbm, v_hbm, w_hbm, out_ref,
    q, kv, stage_q, stage_kv, rq, rkv, own_sum, summ, near, far, ret_out, ret, att_out, att, wbuf,
    in_sem, halo_sem, q_send, q_recv, kv_send, kv_recv, pair_send, pair_recv,
    sz_send, sz_recv, sx_send, sx_recv, sp_send, sp_recv,
    wz_send, wz_recv, wy_send, wy_recv, wx_send, wx_recv, wp_send, wp_recv,
    r_send, r_recv, own_sem, a_send, a_recv,
):
    c = lax.axis_index("ctx")
    h = lax.axis_index("head")
    core, x, zh = c % 2, (c // 2) % 4, c // 8
    zl, y = h % 2, h // 2
    chip = zh * 4 + x
    sib = (c + 1 - 2 * core, h)
    sends = []

    def remote(src, dst, ssem, rsem, dev):
        return pltpu.make_async_remote_copy(
            src_ref=src, dst_ref=dst, send_sem=ssem, recv_sem=rsem,
            device_id=dev, device_id_type=MESH,
        )

    def go(src, dst, ssem, rsem, dev):
        copy = remote(src, dst, ssem, rsem, dev)
        copy.start()
        sends.append(copy)

    def got(ref, sem):
        remote(ref, ref, sem, sem, sib).wait_recv()

    def chip_at(dz, dx):
        return ((zh + dz) % 4) * 4 + (x + dx) % 4

    def source(dz, dx):
        return ((zh - dz + 4) % 4) * 4 + (x - dx + 4) % 4

    def half_block(i):
        return (y // 4 + SHIFTS[i]) % 2

    def block(i):
        return 2 * half_block(i // 2) + i % 2

    offs = [(dz, dx) for dz in (2, 1, 3, 0) for dx in (2, 1, 3, 0) if dz or dx]
    octs = [(a, b) for a in (2, 1, 3, 0) for b in (1, 0)]

    loads = [
        pltpu.make_async_copy(k_hbm, kv.at[0, pl.ds(WINDOW, TOKENS)], in_sem.at[1]),
        pltpu.make_async_copy(v_hbm, kv.at[1, pl.ds(WINDOW, TOKENS)], in_sem.at[2]),
        pltpu.make_async_copy(q_hbm, q, in_sem.at[0]),
        pltpu.make_async_copy(w_hbm, wbuf.at[h], in_sem.at[3]),
    ]
    for load in loads:
        load.start()

    barrier = pltpu.get_barrier_semaphore()

    def greet(dev):
        pl.semaphore_signal(barrier, inc=1, device_id=dev, device_id_type=MESH)

    zfar = (((zh + 2 * zl - 1 + 4) % 4) * 8 + x * 2 + core, 2 * y + 1 - zl)
    zpeer = (c, 2 * y + 1 - zl)
    for dz, dx in offs:
        greet((chip_at(dz, dx) * 2 + core, h))
    for dy in (4, 3, 5, 2, 6, 1, 7, 0):
        for dz in (1, 0):
            if dy or dz:
                greet((c, ((y + dy) % 8) * 2 + (zl + dz) % 2))
    greet(((c + 2 * core - 1) % 32, h))
    greet(zfar)
    greet(sib)

    for load in loads[:2]:
        load.wait()

    ri, ci = iota((256, 256), 0), iota((256, 256), 1)
    swap = jnp.where(((ri >> 4) == (ci & 15)) & ((ri & 15) == (ci >> 4)), 1.0, 0.0).astype(BF16)
    for n in range(2):
        parts = [
            kv[n, pl.ds(WINDOW + 128 * g + 112, 16), :].astype(F32)[8:] for g in range(8)
        ]
        own_sum[n] = jnp.concatenate(parts, axis=0).astype(BF16)
        for b in range(4):
            rows = kv[n, pl.ds(WINDOW + 256 * b, 256), :]
            moved = jnp.dot(swap, rows, preferred_element_type=F32).astype(BF16)
            stage_kv[:, n, pl.ds(16 * b, 16), :] = moved.reshape(CHIPS, 16, HEAD_SIZE)
    rr, cc = iota((LT, SPAN), 0), iota((LT, SPAN), 1)

    def local_tile(i, bias):
        rows = pl.ds(pl.multiple_of(i * LT, LT), LT)
        window = pl.ds(pl.multiple_of(i * LT, LT), SPAN)
        s = scores(q[rows, :], kv[0, window, :])
        allowed = (cc > rr) & (cc <= rr + WINDOW)
        if bias:
            start = jnp.where(c == 0, WINDOW - i * LT, 0)
            allowed = allowed & (cc >= start)
        s = jnp.where(allowed, s, NEG)
        top = jnp.max(s, axis=-1, keepdims=True)
        p = jnp.exp2((s - top) * LOGIT)
        total = jnp.sum(p, axis=-1, keepdims=True)
        near[rows, :] = mix(p, kv[1, window, :]) / total

    half = WINDOW // LT

    pl.semaphore_wait(barrier, 33)

    STEP = (1, 7)
    side = x % 2
    xnext = (zh * 8 + (x + 1 - 2 * side) * 2 + core, h)

    xother = (zh * 8 + ((x + 2 * side + 3) % 4) * 2 + core, h)

    def w_piece(yy, kind, k, p):
        zz = zl if kind == 0 else 1 - zl
        start = pl.multiple_of(64 * k + PART * ((side + p) % 2), PART)
        return wbuf.at[2 * (yy % 8) + zz, pl.ds(start, PART), :]

    orders = [
        [
            (kind, s, p)
            for s in range(4)
            for kind in range(2)
            for p in range(1 if s else 2)
            if s < 3 or kind == d
        ]
        for d in range(2)
    ]
    place = [{key: n for n, key in enumerate(orders[d])} for d in range(2)]
    distant = [(d, key) for d in range(2) for key in orders[d] if key[1]]
    w_count = len(orders[0])

    def w_send(d, key):
        kind, s, p = key
        ref = w_piece(y + (8 - STEP[d]) * s, kind, core, p)
        n = place[d][key]
        go(ref, ref, wy_send.at[d, n], wy_recv.at[d, n], (c, 2 * ((y + STEP[d]) % 8) + zl))

    def w_pair(ref, n):
        go(ref, ref, wp_send.at[n], wp_recv.at[n], sib)

    def w_got(d, key, k, other=0):
        kind, s, p = key
        return w_piece(y + (8 - STEP[d]) * (s + 1), kind, k, p + other)

    def w_relay(*numbers):
        for n in numbers:
            for d in range(2):
                key = orders[d][n]
                kind, s, p = key
                ref = w_got(d, key, core)
                got(ref, wy_recv.at[d, n])
                if (kind, s + 1, p) in place[d]:
                    w_send(d, (kind, s + 1, p))
                if s:
                    m = distant.index((d, key))
                    go(ref, ref, wx_send.at[m], wx_recv.at[m], xnext if s > 1 else xother)
                w_pair(ref, 2 + w_count * d + n)

    def w_cross(*numbers):
        for m in numbers:
            ref = w_got(*distant[m], core, 1)
            got(ref, wx_recv.at[m])
            w_pair(ref, 2 + 2 * w_count + m)

    def w_swap():
        for p, dev in enumerate((zpeer, zfar)):
            start = pl.multiple_of(64 * core + PART * p, PART)
            ref = wbuf.at[h, pl.ds(start, PART), :]
            go(ref, ref, wz_send.at[p], wz_recv.at[p], dev)

    def w_other_part(p, k):
        return wbuf.at[2 * y + 1 - zl, pl.ds(pl.multiple_of(64 * k + PART * p, PART), PART), :]

    def w_other():
        for p in range(2):
            ref = w_other_part(p, core)
            got(ref, wz_recv.at[p])
            w_pair(ref, p)
        for p in range(2):
            w_send(0, (1, 0, p))
            w_send(1, (1, 0, p))

    def w_finish():
        for p in range(2):
            got(w_other_part(p, 1 - core), wp_recv.at[p])
        for d in range(2):
            for n, key in enumerate(orders[d]):
                got(w_got(d, key, 1 - core), wp_recv.at[2 + w_count * d + n])
        for m, (d, key) in enumerate(distant):
            got(w_got(d, key, 1 - core, 1), wp_recv.at[2 + 2 * w_count + m])

    for n, dz in enumerate((2, 1, 3)):
        dev = (((zh + dz) % 4) * 8 + x * 2 + core, h)
        go(own_sum, summ.at[:, zh, x, core], sz_send.at[n], sz_recv.at[n], dev)
    loads[3].wait()
    w_swap()
    for p in range(2):
        w_send(0, (0, 0, p))
        w_send(1, (0, 0, p))
    loads[2].wait()
    for b in range(4):
        moved = jnp.dot(swap, q[pl.ds(256 * b, 256), :], preferred_element_type=F32).astype(BF16)
        stage_q[:, pl.ds(16 * b, 16), :] = moved.reshape(CHIPS, 16, HEAD_SIZE)
    for n, (dz, dx) in enumerate(offs):
        to = chip_at(dz, dx)
        go(stage_kv.at[to], rkv.at[:, chip, core], kv_send.at[n], kv_recv.at[n], (to * 2 + core, h))
    for n, (dz, dx) in enumerate(offs):
        to = chip_at(dz, dx)
        go(stage_q.at[to], rq.at[chip], q_send.at[n], q_recv.at[n], (to * 2 + core, h))
    halo_to = kv.at[:, pl.ds(0, WINDOW)]
    go(kv.at[:, pl.ds(TOKENS, WINDOW)], halo_to, halo_sem.at[0], halo_sem.at[1], ((c + 1) % 32, h))
    own = [
        pltpu.make_async_copy(stage_kv.at[chip], rkv.at[:, chip, core], in_sem.at[4]),
        pltpu.make_async_copy(stage_q.at[chip], rq.at[chip], in_sem.at[5]),
        pltpu.make_async_copy(own_sum, summ.at[:, zh, x, core], in_sem.at[6]),
    ]
    for copy in own:
        copy.start()
    go(stage_kv.at[chip], rkv.at[:, chip, core], pair_send.at[15], pair_recv.at[15], sib)

    @pl.loop(half, TOKENS // LT)
    def _(i):
        local_tile(i, False)

    def take_pairs(numbers):
        for n in numbers:
            ref = rkv.at[:, source(*offs[n]), core]
            got(ref, kv_recv.at[n])
            go(ref, ref, pair_send.at[n], pair_recv.at[n], sib)

    qrow = iota((256, 512), 0)
    kcol = iota((256, 512), 1)

    def summary_tile(i):
        b = block(i)
        rows = pl.ds(pl.multiple_of(b * 256, 256), 256)
        qs = q[rows, :]
        own_rows = pl.ds(pl.multiple_of(WINDOW + b * 256, 256), 256)
        ks = kv[0, own_rows, :].astype(F32)
        vs = kv[1, own_rows, :].astype(F32)
        self_score = jnp.sum(qs.astype(F32) * ks, axis=-1, keepdims=True)
        apart = (iota((256, 1), 0) & 127) < 120
        state = (
            jnp.where(apart, self_score, NEG),
            jnp.where(apart, 1.0, 0.0),
            jnp.where(apart, vs, 0.0),
        )

        def step(t, state):
            return fold(
                qs, summ[0, t].reshape(512, HEAD_SIZE), summ[1, t].reshape(512, HEAD_SIZE), state
            )

        state = lax.fori_loop(0, zh, step, state)
        at = qrow + (b * 256 + (2 * x + core) * TOKENS)
        key_at = (kcol >> 3) * 128 + 120 + (kcol & 7)
        state = fold(
            qs, summ[0, zh].reshape(512, HEAD_SIZE), summ[1, zh].reshape(512, HEAD_SIZE),
            state, key_at <= at,
        )
        far[rows, :] = state[2] / state[1]

    def summary_spread():
        own[2].wait()
        for n, dz in enumerate((2, 1, 3)):
            got(summ.at[:, (zh - dz + 4) % 4, x, core], sz_recv.at[n])
        ref = summ.at[:, :, x, core]
        for n, dx in enumerate((2, 1, 3)):
            dev = (zh * 8 + ((x + dx) % 4) * 2 + core, h)
            go(ref, ref, sx_send.at[n], sx_recv.at[n], dev)
        go(ref, ref, sp_send.at[3], sp_recv.at[3], sib)

    def summary_pair():
        for n, dx in enumerate((2, 1, 3)):
            ref = summ.at[:, :, (x - dx + 4) % 4, core]
            got(ref, sx_recv.at[n])
            go(ref, ref, sp_send.at[n], sp_recv.at[n], sib)

    def summary_ready():
        for n, dx in enumerate((2, 1, 3, 0)):
            got(summ.at[:, :, (x - dx + 4) % 4, 1 - core], sp_recv.at[n])

    def strided_ready():
        own[0].wait()
        own[1].wait()
        for n in range(15):
            got(rkv.at[:, source(*offs[n]), 1 - core], pair_recv.at[n])
        got(rkv.at[:, chip, 1 - core], pair_recv.at[15])
        for n in range(15):
            got(rq.at[source(*offs[n])], q_recv.at[n])

    drow, dcol = iota((64, 512), 0), iota((64, 512), 1)

    def strided_rows(i, u):
        b = 2 * half_block(i) + u
        qs = rq[:, pl.ds(pl.multiple_of(16 * b, 16), 16), :].reshape(256, HEAD_SIZE)
        allowed = dcol <= (drow >> 4) * 128 + (drow & 15) + (core * 64 + b * 16)
        state = None
        for t in range(4):
            ks = rkv[0, pl.ds(t * 4, 4)].reshape(512, HEAD_SIZE)
            vs = rkv[1, pl.ds(t * 4, 4)].reshape(512, HEAD_SIZE)
            s = scores(qs[64 * t :], ks)
            first = jnp.where(allowed, s[:64], NEG)
            s = first if t == 3 else jnp.concatenate([first, s[64:]], axis=0)
            top = jnp.max(s, axis=-1, keepdims=True)
            if t:
                top = jnp.maximum(top, state[0])
            p = jnp.exp2((s - top) * LOGIT)
            total = jnp.sum(p, axis=-1, keepdims=True)
            acc = mix(p, vs)
            if t:
                shrink = jnp.exp2((state[0] - top) * LOGIT)
                total = total + shrink * state[1]
                acc = acc + shrink * state[2]
            done = (acc[:64] / total[:64]).astype(BF16)
            ret_out[i, pl.ds(4 * t, 4), pl.ds(16 * u, 16)] = done.reshape(4, 16, HEAD_SIZE)
            if t < 3:
                state = (top[64:], total[64:], acc[64:])

    def stride_block(i):
        for u in range(2):
            strided_rows(i, u)
        for n, (dz, dx) in enumerate(offs):
            to = chip_at(dz, dx)
            go(ret_out.at[i, to], ret.at[i, chip], r_send.at[i, n], r_recv.at[i, n], (to * 2 + core, h))
        pltpu.make_async_copy(ret_out.at[i, chip], ret.at[i, chip], own_sem.at[i]).start()

    def join_block(i):
        pltpu.make_async_copy(ret_out.at[i, chip], ret.at[i, chip], own_sem.at[i]).wait()
        for n in range(15):
            got(ret.at[i, source(*offs[n])], r_recv.at[i, n])
        for u in range(2):
            rows = pl.ds(pl.multiple_of((2 * half_block(i) + u) * 256, 256), 256)
            part = ret[i, :, pl.ds(16 * u, 16), :].reshape(256, HEAD_SIZE)
            strided = jnp.dot(swap, part, preferred_element_type=F32)
            att_out[i, pl.ds(256 * u, 256), :] = (near[rows, :] + far[rows, :] + strided).astype(BF16)
        for m, (dy, dz) in enumerate(octs):
            yy, zz = (y + dy) % 4, (zl + dz) % 2
            part = att_out.at[i, pl.ds(pl.multiple_of(64 * (2 * yy + zz), 64), 64)]
            if SHIFTS[i] or dy or dz:
                dev = (c, 8 * half_block(i) + 2 * yy + zz)
                go(part, att.at[h], a_send.at[i, m], a_recv.at[i, m], dev)
            else:
                pltpu.make_async_copy(part, att.at[h], own_sem.at[2]).start()

    def attended_ready():
        for i in range(2):
            for m, (dy, dz) in enumerate(octs):
                src = 8 * half_block(i) + 2 * ((y - dy + 4) % 4) + (zl + dz) % 2
                if SHIFTS[i] or dy or dz:
                    got(att.at[src], a_recv.at[i, m])
                else:
                    pltpu.make_async_copy(att.at[src], att.at[src], own_sem.at[2]).wait()

    w_other()
    w_relay(0)
    summary_spread()
    w_relay(1, 2)
    summary_pair()
    w_relay(3)
    take_pairs(range(0, 8))
    w_relay(4)
    take_pairs(range(8, 15))
    w_relay(5)
    strided_ready()
    stride_block(0)
    w_relay(6)
    stride_block(1)
    w_relay(7)
    summary_ready()
    summary_tile(0)
    summary_tile(1)
    w_relay(8)
    summary_tile(2)
    summary_tile(3)
    got(halo_to, halo_sem.at[1])

    @pl.loop(0, half)
    def _(i):
        local_tile(i, True)

    join_block(0)
    w_cross(0, 5, 1, 6, 2, 7)
    join_block(1)
    w_cross(3, 8, 4, 9)
    attended_ready()
    w_finish()

    rows = jnp.concatenate([att[i] for i in range(16)], axis=-1)

    @pl.loop(0, 4)
    def _(n):
        cols = pl.ds(pl.multiple_of(n * 512, 512), 512)
        weights = wbuf[:, :, cols].reshape(2048, 512)
        out_ref[:, cols] = jnp.dot(rows, weights, preferred_element_type=F32)

    for copy in sends:
        copy.wait_send()


def body(queries, keys, values, out_weight):
    dma = pltpu.SemaphoreType.DMA
    wide = (CHIPS, 32, HEAD_SIZE)
    return pl.pallas_call(
        kernel,
        out_shape=jax.ShapeDtypeStruct((64, 2048), F32),
        in_specs=[pl.BlockSpec(memory_space=pl.ANY)] * 4,
        out_specs=pl.BlockSpec(memory_space=pltpu.VMEM),
        scratch_shapes=[
            pltpu.VMEM((TOKENS, HEAD_SIZE), BF16),
            pltpu.VMEM((2, WINDOW + TOKENS, HEAD_SIZE), BF16),
            pltpu.VMEM((CHIPS, ROWS, HEAD_SIZE), BF16),
            pltpu.VMEM((CHIPS, 2, ROWS, HEAD_SIZE), BF16),
            pltpu.VMEM((CHIPS, ROWS, HEAD_SIZE), BF16),
            pltpu.VMEM((2, CHIPS, 2, ROWS, HEAD_SIZE), BF16),
            pltpu.VMEM((2, ROWS, HEAD_SIZE), BF16),
            pltpu.VMEM((2, 4, 4, 2, ROWS, HEAD_SIZE), BF16),
            pltpu.VMEM((TOKENS, HEAD_SIZE), F32),
            pltpu.VMEM((TOKENS, HEAD_SIZE), F32),
            pltpu.VMEM((2, *wide), BF16),
            pltpu.VMEM((2, *wide), BF16),
            pltpu.VMEM((2, 512, HEAD_SIZE), BF16),
            pltpu.VMEM((16, 64, HEAD_SIZE), BF16),
            pltpu.VMEM((16, HEAD_SIZE, 2048), BF16),
            dma((7,)), dma((2,)), dma((15,)), dma((15,)), dma((15,)), dma((15,)),
            dma((16,)), dma((16,)),
            dma((3,)), dma((3,)), dma((3,)), dma((3,)), dma((4,)), dma((4,)),
            dma((2,)), dma((2,)), dma((2, 9)), dma((2, 9)), dma((10,)), dma((10,)),
            dma((30,)), dma((30,)),
            dma((2, 15)), dma((2, 15)), dma((3,)), dma((2, 8)), dma((2, 8)),
        ],
        compiler_params=pltpu.CompilerParams(collective_id=0, has_side_effects=True),
    )(queries, keys, values, out_weight).astype(BF16)


def solution(mesh):
    placed = (P("ctx", "head"), P("ctx", "head"), P("ctx", "head"), P("head", None))
    return jax.shard_map(
        body, mesh=mesh, in_specs=placed, out_specs=P(("ctx", "head"), None), check_vma=False
    )
```

```python
import functools
import math

import jax
import jax.numpy as jnp
from jax import lax
from jax.experimental import pallas as pl
from jax.experimental.pallas import tpu as pltpu
from jax.sharding import PartitionSpec as P

MESH = pl.DeviceIdType.MESH
NEG = -1e30
HEAD_SIZE = 128
WINDOW = 512
LOGIT = math.log2(math.e) * HEAD_SIZE ** -0.5
F32 = jnp.float32
BF16 = jnp.bfloat16
TOKENS = 1024
CHIPS = 16
ROWS = 64
LT = 256
SPAN = LT + WINDOW


def scores(q, k):
    return lax.dot_general(q, k, (((1,), (1,)), ((), ())), preferred_element_type=F32)


def mix(p, v):
    return jnp.dot(p.astype(BF16), v, preferred_element_type=F32)


def fold(q, k, v, state, allowed=None):
    top, total, acc = state
    s = scores(q, k)
    if allowed is not None:
        s = jnp.where(allowed, s, NEG)
    new_top = jnp.maximum(top, jnp.max(s, axis=-1, keepdims=True))
    p = jnp.exp2((s - new_top) * LOGIT)
    shrink = jnp.exp2((top - new_top) * LOGIT)
    total = shrink * total + jnp.sum(p, axis=-1, keepdims=True)
    acc = shrink * acc + mix(p, v)
    return new_top, total, acc


def iota(shape, dim):
    return lax.broadcasted_iota(jnp.int32, shape, dim)


SHIFTS = (1, 0)
PART = 32


def kernel(
    q_hbm, k_hbm, v_hbm, w_hbm, out_ref,
    q, kv, stage_q, stage_kv, rq, rkv, own_sum, summ, near, far, ret_out, ret, att_out, att, wbuf,
    in_sem, halo_sem, q_send, q_recv, kv_send, kv_recv, pair_send, pair_recv,
    sz_send, sz_recv, sx_send, sx_recv, sp_send, sp_recv,
    wz_send, wz_recv, wy_send, wy_recv, wx_send, wx_recv, wp_send, wp_recv,
    r_send, r_recv, own_sem, a_send, a_recv,
):
    c = lax.axis_index("ctx")
    h = lax.axis_index("head")
    core, x, zh = c % 2, (c // 2) % 4, c // 8
    zl, y = h % 2, h // 2
    chip = zh * 4 + x
    sib = (c + 1 - 2 * core, h)
    sends = []

    def remote(src, dst, ssem, rsem, dev):
        return pltpu.make_async_remote_copy(
            src_ref=src, dst_ref=dst, send_sem=ssem, recv_sem=rsem,
            device_id=dev, device_id_type=MESH,
        )

    def go(src, dst, ssem, rsem, dev):
        copy = remote(src, dst, ssem, rsem, dev)
        copy.start()
        sends.append(copy)

    def got(ref, sem):
        remote(ref, ref, sem, sem, sib).wait_recv()

    def chip_at(dz, dx):
        return ((zh + dz) % 4) * 4 + (x + dx) % 4

    def source(dz, dx):
        return ((zh - dz + 4) % 4) * 4 + (x - dx + 4) % 4

    def half_block(i):
        return (y // 4 + SHIFTS[i]) % 2

    def block(i):
        return 2 * half_block(i // 2) + i % 2

    offs = [(dz, dx) for dz in (2, 1, 3, 0) for dx in (2, 1, 3, 0) if dz or dx]
    octs = [(a, b) for a in (2, 1, 3, 0) for b in (1, 0)]

    loads = [
        pltpu.make_async_copy(k_hbm, kv.at[0, pl.ds(WINDOW, TOKENS)], in_sem.at[1]),
        pltpu.make_async_copy(v_hbm, kv.at[1, pl.ds(WINDOW, TOKENS)], in_sem.at[2]),
        pltpu.make_async_copy(q_hbm, q, in_sem.at[0]),
        pltpu.make_async_copy(w_hbm, wbuf.at[h], in_sem.at[3]),
    ]
    for load in loads:
        load.start()

    barrier = pltpu.get_barrier_semaphore()

    def greet(dev):
        pl.semaphore_signal(barrier, inc=1, device_id=dev, device_id_type=MESH)

    zfar = (((zh + 2 * zl - 1 + 4) % 4) * 8 + x * 2 + core, 2 * y + 1 - zl)
    zpeer = (c, 2 * y + 1 - zl)
    for dz, dx in offs:
        greet((chip_at(dz, dx) * 2 + core, h))
    for dy in (4, 3, 5, 2, 6, 1, 7, 0):
        for dz in (1, 0):
            if dy or dz:
                greet((c, ((y + dy) % 8) * 2 + (zl + dz) % 2))
    greet(((c + 2 * core - 1) % 32, h))
    greet(zfar)
    greet(sib)

    for load in loads[:2]:
        load.wait()

    ri, ci = iota((256, 256), 0), iota((256, 256), 1)
    swap = jnp.where(((ri >> 4) == (ci & 15)) & ((ri & 15) == (ci >> 4)), 1.0, 0.0).astype(BF16)
    for n in range(2):
        parts = [
            kv[n, pl.ds(WINDOW + 128 * g + 112, 16), :].astype(F32)[8:] for g in range(8)
        ]
        own_sum[n] = jnp.concatenate(parts, axis=0).astype(BF16)
        for b in range(4):
            rows = kv[n, pl.ds(WINDOW + 256 * b, 256), :]
            moved = jnp.dot(swap, rows, preferred_element_type=F32).astype(BF16)
            stage_kv[:, n, pl.ds(16 * b, 16), :] = moved.reshape(CHIPS, 16, HEAD_SIZE)
    rr, cc = iota((LT, SPAN), 0), iota((LT, SPAN), 1)

    def local_tile(i, bias):
        rows = pl.ds(pl.multiple_of(i * LT, LT), LT)
        window = pl.ds(pl.multiple_of(i * LT, LT), SPAN)
        s = scores(q[rows, :], kv[0, window, :])
        allowed = (cc > rr) & (cc <= rr + WINDOW)
        if bias:
            start = jnp.where(c == 0, WINDOW - i * LT, 0)
            allowed = allowed & (cc >= start)
        s = jnp.where(allowed, s, NEG)
        top = jnp.max(s, axis=-1, keepdims=True)
        p = jnp.exp2((s - top) * LOGIT)
        total = jnp.sum(p, axis=-1, keepdims=True)
        near[rows, :] = mix(p, kv[1, window, :]) / total

    half = WINDOW // LT

    pl.semaphore_wait(barrier, 33)

    STEP = (1, 7)
    side = x % 2
    xnext = (zh * 8 + (x + 1 - 2 * side) * 2 + core, h)

    xother = (zh * 8 + ((x + 2 * side + 3) % 4) * 2 + core, h)

    def w_piece(yy, kind, k, p):
        zz = zl if kind == 0 else 1 - zl
        start = pl.multiple_of(64 * k + PART * ((side + p) % 2), PART)
        return wbuf.at[2 * (yy % 8) + zz, pl.ds(start, PART), :]

    orders = [
        [
            (kind, s, p)
            for s in range(4)
            for kind in range(2)
            for p in range(1 if s else 2)
            if s < 3 or kind == d
        ]
        for d in range(2)
    ]
    place = [{key: n for n, key in enumerate(orders[d])} for d in range(2)]
    distant = [(d, key) for d in range(2) for key in orders[d] if key[1]]
    w_count = len(orders[0])

    def w_send(d, key):
        kind, s, p = key
        ref = w_piece(y + (8 - STEP[d]) * s, kind, core, p)
        n = place[d][key]
        go(ref, ref, wy_send.at[d, n], wy_recv.at[d, n], (c, 2 * ((y + STEP[d]) % 8) + zl))

    def w_pair(ref, n):
        go(ref, ref, wp_send.at[n], wp_recv.at[n], sib)

    def w_got(d, key, k, other=0):
        kind, s, p = key
        return w_piece(y + (8 - STEP[d]) * (s + 1), kind, k, p + other)

    def w_relay(*numbers):
        for n in numbers:
            for d in range(2):
                key = orders[d][n]
                kind, s, p = key
                ref = w_got(d, key, core)
                got(ref, wy_recv.at[d, n])
                if (kind, s + 1, p) in place[d]:
                    w_send(d, (kind, s + 1, p))
                if s:
                    m = distant.index((d, key))
                    go(ref, ref, wx_send.at[m], wx_recv.at[m], xnext if s > 1 else xother)
                w_pair(ref, 2 + w_count * d + n)

    def w_cross(*numbers):
        for m in numbers:
            ref = w_got(*distant[m], core, 1)
            got(ref, wx_recv.at[m])
            w_pair(ref, 2 + 2 * w_count + m)

    def w_swap():
        for p, dev in enumerate((zpeer, zfar)):
            start = pl.multiple_of(64 * core + PART * p, PART)
            ref = wbuf.at[h, pl.ds(start, PART), :]
            go(ref, ref, wz_send.at[p], wz_recv.at[p], dev)

    def w_other_part(p, k):
        return wbuf.at[2 * y + 1 - zl, pl.ds(pl.multiple_of(64 * k + PART * p, PART), PART), :]

    def w_other():
        for p in range(2):
            ref = w_other_part(p, core)
            got(ref, wz_recv.at[p])
            w_pair(ref, p)
        for p in range(2):
            w_send(0, (1, 0, p))
            w_send(1, (1, 0, p))

    def w_finish():
        for p in range(2):
            got(w_other_part(p, 1 - core), wp_recv.at[p])
        for d in range(2):
            for n, key in enumerate(orders[d]):
                got(w_got(d, key, 1 - core), wp_recv.at[2 + w_count * d + n])
        for m, (d, key) in enumerate(distant):
            got(w_got(d, key, 1 - core, 1), wp_recv.at[2 + 2 * w_count + m])

    for n, dz in enumerate((2, 1, 3)):
        dev = (((zh + dz) % 4) * 8 + x * 2 + core, h)
        go(own_sum, summ.at[:, zh, x, core], sz_send.at[n], sz_recv.at[n], dev)
    loads[3].wait()
    w_swap()
    for p in range(2):
        w_send(0, (0, 0, p))
        w_send(1, (0, 0, p))
    loads[2].wait()
    for b in range(4):
        moved = jnp.dot(swap, q[pl.ds(256 * b, 256), :], preferred_element_type=F32).astype(BF16)
        stage_q[:, pl.ds(16 * b, 16), :] = moved.reshape(CHIPS, 16, HEAD_SIZE)
    for n, (dz, dx) in enumerate(offs):
        to = chip_at(dz, dx)
        go(stage_kv.at[to], rkv.at[:, chip, core], kv_send.at[n], kv_recv.at[n], (to * 2 + core, h))
    for n, (dz, dx) in enumerate(offs):
        to = chip_at(dz, dx)
        go(stage_q.at[to], rq.at[chip], q_send.at[n], q_recv.at[n], (to * 2 + core, h))
    halo_to = kv.at[:, pl.ds(0, WINDOW)]
    go(kv.at[:, pl.ds(TOKENS, WINDOW)], halo_to, halo_sem.at[0], halo_sem.at[1], ((c + 1) % 32, h))
    own = [
        pltpu.make_async_copy(stage_kv.at[chip], rkv.at[:, chip, core], in_sem.at[4]),
        pltpu.make_async_copy(stage_q.at[chip], rq.at[chip], in_sem.at[5]),
        pltpu.make_async_copy(own_sum, summ.at[:, zh, x, core], in_sem.at[6]),
    ]
    for copy in own:
        copy.start()
    go(stage_kv.at[chip], rkv.at[:, chip, core], pair_send.at[15], pair_recv.at[15], sib)

    @pl.loop(half, TOKENS // LT)
    def _(i):
        local_tile(i, False)

    def take_pairs(numbers):
        for n in numbers:
            ref = rkv.at[:, source(*offs[n]), core]
            got(ref, kv_recv.at[n])
            go(ref, ref, pair_send.at[n], pair_recv.at[n], sib)

    qrow = iota((256, 512), 0)
    kcol = iota((256, 512), 1)

    def summary_tile(i):
        b = block(i)
        rows = pl.ds(pl.multiple_of(b * 256, 256), 256)
        qs = q[rows, :]
        own_rows = pl.ds(pl.multiple_of(WINDOW + b * 256, 256), 256)
        ks = kv[0, own_rows, :].astype(F32)
        vs = kv[1, own_rows, :].astype(F32)
        self_score = jnp.sum(qs.astype(F32) * ks, axis=-1, keepdims=True)
        apart = (iota((256, 1), 0) & 127) < 120
        state = (
            jnp.where(apart, self_score, NEG),
            jnp.where(apart, 1.0, 0.0),
            jnp.where(apart, vs, 0.0),
        )

        def step(t, state):
            return fold(
                qs, summ[0, t].reshape(512, HEAD_SIZE), summ[1, t].reshape(512, HEAD_SIZE), state
            )

        state = lax.fori_loop(0, zh, step, state)
        at = qrow + (b * 256 + (2 * x + core) * TOKENS)
        key_at = (kcol >> 3) * 128 + 120 + (kcol & 7)
        state = fold(
            qs, summ[0, zh].reshape(512, HEAD_SIZE), summ[1, zh].reshape(512, HEAD_SIZE),
            state, key_at <= at,
        )
        far[rows, :] = state[2] / state[1]

    def summary_spread():
        own[2].wait()
        for n, dz in enumerate((2, 1, 3)):
            got(summ.at[:, (zh - dz + 4) % 4, x, core], sz_recv.at[n])
        ref = summ.at[:, :, x, core]
        for n, dx in enumerate((2, 1, 3)):
            dev = (zh * 8 + ((x + dx) % 4) * 2 + core, h)
            go(ref, ref, sx_send.at[n], sx_recv.at[n], dev)
        go(ref, ref, sp_send.at[3], sp_recv.at[3], sib)

    def summary_pair():
        for n, dx in enumerate((2, 1, 3)):
            ref = summ.at[:, :, (x - dx + 4) % 4, core]
            got(ref, sx_recv.at[n])
            go(ref, ref, sp_send.at[n], sp_recv.at[n], sib)

    def summary_ready():
        for n, dx in enumerate((2, 1, 3, 0)):
            got(summ.at[:, :, (x - dx + 4) % 4, 1 - core], sp_recv.at[n])

    def strided_ready():
        own[0].wait()
        own[1].wait()
        for n in range(15):
            got(rkv.at[:, source(*offs[n]), 1 - core], pair_recv.at[n])
        got(rkv.at[:, chip, 1 - core], pair_recv.at[15])
        for n in range(15):
            got(rq.at[source(*offs[n])], q_recv.at[n])

    drow, dcol = iota((64, 512), 0), iota((64, 512), 1)

    def strided_rows(i, u):
        b = 2 * half_block(i) + u
        qs = rq[:, pl.ds(pl.multiple_of(16 * b, 16), 16), :].reshape(256, HEAD_SIZE)
        allowed = dcol <= (drow >> 4) * 128 + (drow & 15) + (core * 64 + b * 16)
        state = None
        for t in range(4):
            ks = rkv[0, pl.ds(t * 4, 4)].reshape(512, HEAD_SIZE)
            vs = rkv[1, pl.ds(t * 4, 4)].reshape(512, HEAD_SIZE)
            s = scores(qs[64 * t :], ks)
            first = jnp.where(allowed, s[:64], NEG)
            s = first if t == 3 else jnp.concatenate([first, s[64:]], axis=0)
            top = jnp.max(s, axis=-1, keepdims=True)
            if t:
                top = jnp.maximum(top, state[0])
            p = jnp.exp2((s - top) * LOGIT)
            total = jnp.sum(p, axis=-1, keepdims=True)
            acc = mix(p, vs)
            if t:
                shrink = jnp.exp2((state[0] - top) * LOGIT)
                total = total + shrink * state[1]
                acc = acc + shrink * state[2]
            done = (acc[:64] / total[:64]).astype(BF16)
            ret_out[i, pl.ds(4 * t, 4), pl.ds(16 * u, 16)] = done.reshape(4, 16, HEAD_SIZE)
            if t < 3:
                state = (top[64:], total[64:], acc[64:])

    def stride_block(i):
        for u in range(2):
            strided_rows(i, u)
        for n, (dz, dx) in enumerate(offs):
            to = chip_at(dz, dx)
            go(ret_out.at[i, to], ret.at[i, chip], r_send.at[i, n], r_recv.at[i, n], (to * 2 + core, h))
        pltpu.make_async_copy(ret_out.at[i, chip], ret.at[i, chip], own_sem.at[i]).start()

    def join_block(i):
        pltpu.make_async_copy(ret_out.at[i, chip], ret.at[i, chip], own_sem.at[i]).wait()
        for n in range(15):
            got(ret.at[i, source(*offs[n])], r_recv.at[i, n])
        for u in range(2):
            rows = pl.ds(pl.multiple_of((2 * half_block(i) + u) * 256, 256), 256)
            part = ret[i, :, pl.ds(16 * u, 16), :].reshape(256, HEAD_SIZE)
            strided = jnp.dot(swap, part, preferred_element_type=F32)
            att_out[i, pl.ds(256 * u, 256), :] = (near[rows, :] + far[rows, :] + strided).astype(BF16)
        for m, (dy, dz) in enumerate(octs):
            yy, zz = (y + dy) % 4, (zl + dz) % 2
            part = att_out.at[i, pl.ds(pl.multiple_of(64 * (2 * yy + zz), 64), 64)]
            if SHIFTS[i] or dy or dz:
                dev = (c, 8 * half_block(i) + 2 * yy + zz)
                go(part, att.at[h], a_send.at[i, m], a_recv.at[i, m], dev)
            else:
                pltpu.make_async_copy(part, att.at[h], own_sem.at[2]).start()

    def attended_ready():
        for i in range(2):
            for m, (dy, dz) in enumerate(octs):
                src = 8 * half_block(i) + 2 * ((y - dy + 4) % 4) + (zl + dz) % 2
                if SHIFTS[i] or dy or dz:
                    got(att.at[src], a_recv.at[i, m])
                else:
                    pltpu.make_async_copy(att.at[src], att.at[src], own_sem.at[2]).wait()

    w_other()
    w_relay(0)
    summary_spread()
    w_relay(1, 2)
    summary_pair()
    w_relay(3)
    take_pairs(range(0, 8))
    w_relay(4)
    take_pairs(range(8, 15))
    w_relay(5)
    strided_ready()
    stride_block(0)
    w_relay(6)
    stride_block(1)
    w_relay(7)
    summary_ready()
    summary_tile(0)
    summary_tile(1)
    w_relay(8)
    got(halo_to, halo_sem.at[1])

    @pl.loop(0, half)
    def _(i):
        local_tile(i, True)

    join_block(0)
    summary_tile(2)
    w_cross(0, 5, 1, 6)
    summary_tile(3)
    w_cross(2, 7)
    join_block(1)
    w_cross(3, 8, 4, 9)
    attended_ready()
    w_finish()

    rows = jnp.concatenate([att[i] for i in range(16)], axis=-1)

    @pl.loop(0, 4)
    def _(n):
        cols = pl.ds(pl.multiple_of(n * 512, 512), 512)
        weights = wbuf[:, :, cols].reshape(2048, 512)
        out_ref[:, cols] = jnp.dot(rows, weights, preferred_element_type=F32)

    for copy in sends:
        copy.wait_send()


def body(queries, keys, values, out_weight):
    dma = pltpu.SemaphoreType.DMA
    wide = (CHIPS, 32, HEAD_SIZE)
    return pl.pallas_call(
        kernel,
        out_shape=jax.ShapeDtypeStruct((64, 2048), F32),
        in_specs=[pl.BlockSpec(memory_space=pl.ANY)] * 4,
        out_specs=pl.BlockSpec(memory_space=pltpu.VMEM),
        scratch_shapes=[
            pltpu.VMEM((TOKENS, HEAD_SIZE), BF16),
            pltpu.VMEM((2, WINDOW + TOKENS, HEAD_SIZE), BF16),
            pltpu.VMEM((CHIPS, ROWS, HEAD_SIZE), BF16),
            pltpu.VMEM((CHIPS, 2, ROWS, HEAD_SIZE), BF16),
            pltpu.VMEM((CHIPS, ROWS, HEAD_SIZE), BF16),
            pltpu.VMEM((2, CHIPS, 2, ROWS, HEAD_SIZE), BF16),
            pltpu.VMEM((2, ROWS, HEAD_SIZE), BF16),
            pltpu.VMEM((2, 4, 4, 2, ROWS, HEAD_SIZE), BF16),
            pltpu.VMEM((TOKENS, HEAD_SIZE), F32),
            pltpu.VMEM((TOKENS, HEAD_SIZE), F32),
            pltpu.VMEM((2, *wide), BF16),
            pltpu.VMEM((2, *wide), BF16),
            pltpu.VMEM((2, 512, HEAD_SIZE), BF16),
            pltpu.VMEM((16, 64, HEAD_SIZE), BF16),
            pltpu.VMEM((16, HEAD_SIZE, 2048), BF16),
            dma((7,)), dma((2,)), dma((15,)), dma((15,)), dma((15,)), dma((15,)),
            dma((16,)), dma((16,)),
            dma((3,)), dma((3,)), dma((3,)), dma((3,)), dma((4,)), dma((4,)),
            dma((2,)), dma((2,)), dma((2, 9)), dma((2, 9)), dma((10,)), dma((10,)),
            dma((30,)), dma((30,)),
            dma((2, 15)), dma((2, 15)), dma((3,)), dma((2, 8)), dma((2, 8)),
        ],
        compiler_params=pltpu.CompilerParams(collective_id=0, has_side_effects=True),
    )(queries, keys, values, out_weight).astype(BF16)


def solution(mesh):
    placed = (P("ctx", "head"), P("ctx", "head"), P("ctx", "head"), P("head", None))
    return jax.shard_map(
        body, mesh=mesh, in_specs=placed, out_specs=P(("ctx", "head"), None), check_vma=False
    )
```
